256 devices in a mesh: energy: 32 (over x, y, core), space: 8 (over z).
Axes of the slice: x: 4, y: 4, z: 8, core: 2. Of those that a mesh axis runs over, the one named last changes fastest.
Arguments:
- g_upper: bfloat16 [2, 128, 8, 384, 384], P(None, 'energy', 'space'), may hold values from -6 to 6
- p_diag: bfloat16 [2, 128, 8, 384, 384], P(None, 'energy', 'space'), may hold values from -0.8984375 to 0.8984375
- p_upper: bfloat16 [2, 128, 8, 384, 384], P(None, 'energy', 'space'), may hold values from -0.8984375 to 0.8984375
- v_diag: bfloat16 [8, 384, 384], P('space'), may hold values from -0.3125 to 0.3125
- v_upper: bfloat16 [8, 384, 384], P('space'), may hold values from -0.3125 to 0.3125
- v_pattern: int32 [8], P('space'), may hold values from 0 to 1, as said below
- element_present: int32 [8, 48], P('space'), may hold values from 0 to 1, as said below
Outputs:
- sigma_upper: bfloat16 [2, 128, 8, 384, 384], P(None, 'energy', 'space')
The draws below stay inside these ranges and needn't reach their ends.
Inputs may be any that keep to these rules, and one draw needn't show every extreme that they name: `element_present`: no block row has more than 30 present groups, and some block row has exactly 30. `v_pattern`: the first and the last block row always have their upper block; the others may lack it.
All inputs are finite; a program needn't handle non-finite values.
Results may differ from the reference program's by a relative error of at most 0.013.
Values may be sent and summed in bfloat16 or wider, within the bound.
No kernel may reach another device: no remote copies, remote signals or barrier semaphores. Data moves between devices by JAX's collectives and lax.ppermute only.
A program may use at most 128 MiB of HBM per device.

```python
import math
import jax
import jax.numpy as jnp
from jax import lax

B = 384
RG = 8
NE = 128
NB = 8
NG = 48
LIVE = 30


def draw_v_pattern(key, part):
    inner_bits = jax.random.randint(jax.random.fold_in(key, 29), (NB,), 0, 2, dtype=jnp.int32)
    positions = jnp.arange(NB, dtype=jnp.int32)
    edges = (positions == 0) | (positions == NB - 1)
    return jnp.where(edges, jnp.ones((NB,), jnp.int32), inner_bits)


def draw_element_present(key, part):
    base = jax.random.fold_in(key, 17)
    counts = jax.random.randint(jax.random.fold_in(base, 1), (NB,), max(NG // 4, 1), LIVE + 1, dtype=jnp.int32)
    fullest = jax.random.randint(jax.random.fold_in(base, 2), (), 0, NB, dtype=jnp.int32)
    counts = jnp.where(jnp.arange(NB, dtype=jnp.int32) == fullest, LIVE, counts)

    def one_row(row_key, count):
        order = jax.random.permutation(row_key, NG).astype(jnp.int32)
        ranks = jnp.zeros((NG,), jnp.int32).at[order].set(jnp.arange(NG, dtype=jnp.int32))
        return (ranks < count).astype(jnp.int32)
    return jax.vmap(one_row)(jax.random.split(jax.random.fold_in(base, 3), NB), counts)


def steps_of(key, shape, shards, low, top_value):
    def one(dim, blocks):
        draws = jax.random.uniform(jax.random.fold_in(jax.random.fold_in(key, 6), dim), (blocks,), jnp.float32, low / len(shards), top_value / len(shards))
        return jnp.repeat(jnp.exp(draws), shape[dim] // blocks).reshape((-1,) + (1,) * (len(shape) - dim - 1))

    level = one(*shards[0])
    for cut in shards[1:]:
        level = level * one(*cut)
    return level


def scatter_about(key, dims, deviation, most, shards=(), kind=jnp.bfloat16):
    array = deviation * jax.random.normal(key, dims, jnp.float32)
    if shards:
        array = array * steps_of(key, dims, shards, -0.22, 0.18)
    return jnp.clip(array, -most, most).astype(kind)


def setup_inputs(seed: int = 0) -> dict:
    arg_keys = jax.random.split(jax.random.key(seed), 8)
    g_upper = scatter_about(arg_keys[0], (2, NE, NB, B, B), 1.0, 6.0, ((1, 32), (2, 8)))
    p_diag = scatter_about(arg_keys[1], (2, NE, NB, B, B), 0.15, 0.8984375, ((1, 32), (2, 8)))
    p_upper = scatter_about(arg_keys[2], (2, NE, NB, B, B), 0.15, 0.8984375, ((1, 32), (2, 8)))
    v_diag = scatter_about(arg_keys[3], (NB, B, B), B ** -0.5, 0.3125, ((0, 8),))
    v_upper = scatter_about(arg_keys[4], (NB, B, B), B ** -0.5, 0.3125, ((0, 8),))
    v_pattern = draw_v_pattern(jax.random.fold_in(arg_keys[7], 71), 0)
    element_present = draw_element_present(jax.random.fold_in(arg_keys[7], 71), 0)
    return dict(g_upper=g_upper, p_diag=p_diag, p_upper=p_upper, v_diag=v_diag, v_upper=v_upper, v_pattern=v_pattern, element_present=element_present)


def rounded(values):
    return lax.optimization_barrier(values.astype(jnp.bfloat16)).astype(jnp.float32)

def reference(g_upper, p_diag, p_upper, v_diag, v_upper, v_pattern, element_present):
    upper_masked = v_upper.astype(jnp.float32) * v_pattern.astype(jnp.float32)[:, None, None]
    square = v_diag.astype(jnp.float32)
    results = []
    for block_row in range(NB):
        previous = (block_row - 1) % NB
        following = (block_row + 1) % NB
        pd_own = p_diag[:, :, block_row].astype(jnp.float32)
        pu_own = p_upper[:, :, block_row].astype(jnp.float32)
        pu_prev = p_upper[:, :, previous].astype(jnp.float32)
        pd_next = p_diag[:, :, following].astype(jnp.float32)
        pu_next = p_upper[:, :, following].astype(jnp.float32)
        vu_own = upper_masked[block_row]
        vu_prev = upper_masked[previous]
        vu_next = upper_masked[following]
        vd_own = square[block_row]
        vd_next = square[following]
        vp_same = rounded(jnp.einsum('ki,cekj->ceij', vu_prev, pu_prev) + jnp.einsum('ik,cekj->ceij', vd_own, pd_own) + jnp.einsum('ik,cejk->ceij', vu_own, pu_own))
        vp_one = rounded(jnp.einsum('ik,cekj->ceij', vd_own, pu_own) + jnp.einsum('ik,cekj->ceij', vu_own, pd_next))
        vp_two = rounded(jnp.einsum('ik,cekj->ceij', vu_own, pu_next))
        screened = jnp.einsum('ceik,kj->ceij', vp_same, vu_own) + jnp.einsum('ceik,kj->ceij', vp_one, vd_next) + jnp.einsum('ceik,jk->ceij', vp_two, vu_next)
        screened = rounded(screened.at[0].add(vu_own))
        green_row = g_upper[:, :, block_row].astype(jnp.float32)
        green_cplx = green_row[0] + 1j * green_row[1]
        screen_cplx = screened[0] + 1j * screened[1]
        folded = jnp.fft.ifft(jnp.fft.fft(green_cplx, axis=0) * jnp.fft.fft(screen_cplx, axis=0), axis=0)
        sigma_row = 1j * folded / math.sqrt(NE)
        kept_rows = jnp.repeat(element_present[block_row].astype(jnp.float32), RG)
        stacked = jnp.stack([jnp.real(sigma_row), jnp.imag(sigma_row)]).astype(jnp.float32) * kept_rows[None, None, :, None]
        results.append(stacked.astype(jnp.bfloat16))
    return jnp.stack(results, axis=2)
```

```python
import functools
import math

import jax
import jax.numpy as jnp
import numpy as np
from jax import lax
from jax.experimental import pallas as pl
from jax.experimental.pallas import tpu as pltpu
from jax.sharding import PartitionSpec as P

LIVE = 30
RG = 8
LANES = 128
CHUNKS = 1

F32 = jnp.float32
BF16 = jnp.bfloat16


def smem():
    return pl.BlockSpec(memory_space=pltpu.SMEM)


def vmem():
    return pl.BlockSpec(memory_space=pltpu.VMEM)


def shifted(value, steps):
    count = lax.axis_size("space")
    pairs = [(source, (source + steps) % count) for source in range(count)]
    return lax.ppermute(value, "space", pairs)


def dot(left, right):
    return lax.dot_general(left, right, (((1,), (0,)), ((), ())), preferred_element_type=F32)


def dot_nt(left, right):
    return lax.dot_general(left, right, (((1,), (1,)), ((), ())), preferred_element_type=F32)


def tables(energies, peers):
    local = energies // peers
    src, half, step = np.meshgrid(np.arange(peers), np.arange(2), np.arange(local), indexing="ij")
    time = (src * local + step).reshape(-1)
    half = half.reshape(-1)
    freq = np.arange(energies)
    angles = 2.0 * math.pi / energies * ((freq[:, None] * time[None, :]) % energies)
    cosine, sine = np.cos(angles), np.sin(angles)
    real_part = np.where(half == 0, cosine, sine)
    imag_part = np.where(half == 0, -sine, cosine)
    forward = np.concatenate([real_part, imag_part], 0)
    real_out = np.concatenate([-sine, -cosine], 0).T
    imag_out = np.concatenate([cosine, -sine], 0).T
    inverse = np.where((half == 0)[:, None], real_out, imag_out)
    return jnp.asarray(forward, BF16), jnp.asarray(inverse, BF16)


def spread(dest_ref, plane, planes, value):
    rows = value.shape[0]
    for j in range(value.shape[1] // LANES):
        dest_ref[j, pl.ds(plane, rows, stride=planes), :] = value[:, j * LANES : (j + 1) * LANES]


def joined(source_ref):
    return jnp.concatenate([source_ref[j] for j in range(source_ref.shape[0])], axis=1)


def live_list(present_ref, idx_ref):
    groups = present_ref.shape[0]

    def clear(slot, carry):
        idx_ref[slot] = 0
        return carry

    lax.fori_loop(0, groups, clear, 0)

    def visit(group, count):
        idx_ref[count] = group
        return count + jnp.where(present_ref[group] > 0, 1, 0)

    return lax.fori_loop(0, groups, visit, 0)


def pick_rows(idx_ref, source_ref, dest_ref):
    def one(slot, carry):
        row = pl.multiple_of(idx_ref[slot] * RG, RG)
        dest_ref[pl.ds(pl.multiple_of(slot * RG, RG), RG), :] = source_ref[pl.ds(row, RG), :]
        return carry

    lax.fori_loop(0, LIVE, one, 0, unroll=5)


def pack_kernel(chunks, present_ref, g_ref, out_ref, idx_ref, turn_ref):
    planes = g_ref.shape[0]
    rows = RG // chunks
    per_chunk = LIVE // chunks
    live_list(present_ref, idx_ref)

    def one(slot, carry):
        row = pl.multiple_of(idx_ref[slot] * RG, RG)
        chunk = slot // per_chunk
        peer = (slot % per_chunk) * chunks
        for plane in range(planes):
            spread(turn_ref, plane, planes, g_ref[plane, pl.ds(row, RG), :].astype(F32))
        value = joined(turn_ref).astype(BF16)
        for part in range(chunks):
            at = part * rows * planes
            out_ref[peer + part, pl.ds(chunk * rows, rows)] = value[at : at + rows * planes].reshape(
                rows, planes, value.shape[1]
            )
        return carry

    lax.fori_loop(0, LIVE, one, 0, unroll=2)
    for peer in range(LIVE, out_ref.shape[0]):
        out_ref[peer] = jnp.zeros(out_ref.shape[1:], BF16)


def forward_kernel(present_ref, pattern_ref, vu_ref, pu_ref, out_ref, idx_ref, turned, picked, total):
    planes = pu_ref.shape[0]
    rows = LIVE * RG
    live_list(present_ref, idx_ref)
    scale = pattern_ref[0].astype(F32)
    turned[...] = vu_ref[...].astype(F32).T * scale
    pick_rows(idx_ref, turned, picked)
    left = picked[...].astype(BF16)

    def one(plane, carry):
        spread(total, plane, planes, dot(left, pu_ref[plane]))
        return carry

    lax.fori_loop(0, planes, one, 0)
    out_ref[...] = joined(total).astype(BF16)


def backward_kernel(
    present_ref, pattern_ref, vu_prev_ref, vd_ref, vu_ref, pd_ref, pu_ref, out_ref, idx_ref, wide, picked, total
):
    planes = pu_ref.shape[0]
    rows = LIVE * RG
    live_list(present_ref, idx_ref)
    wide[...] = vu_prev_ref[...].astype(F32)
    pick_rows(idx_ref, wide, picked)
    left = picked[...].astype(BF16)
    scale = pattern_ref[0].astype(F32)
    masked = (vu_ref[...].astype(F32) * scale).astype(BF16)

    def one(plane, carry):
        inner = dot(pd_ref[plane], vd_ref[...]) + dot_nt(pu_ref[plane], masked)
        spread(total, plane, planes, dot(left, inner.astype(BF16)))
        return carry

    lax.fori_loop(0, planes, one, 0)
    out_ref[...] = joined(total).astype(BF16)


def local_kernel(
    present_ref,
    pattern_ref,
    vu_ref,
    vd_ref,
    vd_next_ref,
    pd_ref,
    pu_ref,
    out_ref,
    idx_ref,
    wide,
    picked_u,
    picked_d,
    same,
    one_up,
    bare,
):
    planes = pu_ref.shape[0]
    rows = LIVE * RG
    live_list(present_ref, idx_ref)
    scale = pattern_ref[0].astype(F32)
    wide[...] = vu_ref[...].astype(F32) * scale
    masked = wide[...].astype(BF16)
    pick_rows(idx_ref, wide, picked_u)
    wide[...] = vd_ref[...].astype(F32)
    pick_rows(idx_ref, wide, picked_d)
    left_u = picked_u[...].astype(BF16)
    left_d = picked_d[...].astype(BF16)

    def one(plane, carry):
        spread(same, plane, planes, dot(left_d, pd_ref[plane]) + dot_nt(left_u, pu_ref[plane]))
        spread(one_up, plane, planes, dot(left_d, pu_ref[plane]))
        where = jnp.where(plane < planes // 2, 1.0, 0.0).astype(F32)
        spread(bare, plane, planes, picked_u[...] * where)
        return carry

    lax.fori_loop(0, planes, one, 0)
    out_ref[...] = (
        joined(bare)
        + dot(joined(same).astype(BF16), masked)
        + dot(joined(one_up).astype(BF16), vd_next_ref[...])
    )


def join_kernel(pattern_ref, local_ref, before_ref, after_ref, vu_ref, out_ref):
    scale = pattern_ref[0].astype(F32)
    masked = (vu_ref[...].astype(F32) * scale).astype(BF16)
    size = local_ref.shape[0]
    out_ref[0:size, :] = (
        local_ref[...] + dot(before_ref[...], masked) + after_ref[...].astype(F32) * scale
    ).astype(BF16)
    out_ref[size:, :] = jnp.zeros((out_ref.shape[0] - size, out_ref.shape[1]), BF16)


def spectrum_kernel(scale, forward_ref, got_ref, out_ref):
    peers, rows, planes, cols = got_ref.shape
    for r in range(rows):
        values = got_ref[:, r].reshape(peers * planes, cols)
        out_ref[r] = dot(forward_ref[...], values) * scale


def convolve_kernel(forward_ref, inverse_ref, green_ref, got_ref, out_ref):
    peers, rows, planes, cols = got_ref.shape
    half = forward_ref.shape[0] // 2
    for r in range(rows):
        values = got_ref[:, r].reshape(peers * planes, cols)
        freq = dot(forward_ref[...], values)
        green = green_ref[r]
        green_re, green_im = green[:half], green[half:]
        screen_re, screen_im = freq[:half], freq[half:]
        mixed = jnp.concatenate(
            [green_re * screen_re - green_im * screen_im, green_re * screen_im + green_im * screen_re], 0
        )
        result = dot(inverse_ref[...], mixed.astype(BF16)).astype(BF16)
        out_ref[:, r] = result.reshape(peers, planes, cols)


def unpack_kernel(chunks, present_ref, *refs):
    got_refs, (out_ref, idx_ref, turn_ref) = refs[:chunks], refs[chunks:]
    planes = out_ref.shape[0]
    per_chunk = LIVE // chunks
    count = live_list(present_ref, idx_ref)
    out_ref[...] = jnp.zeros(out_ref.shape, BF16)
    for chunk, got_ref in enumerate(got_refs):

        def one(slot, carry, got_ref=got_ref, chunk=chunk):
            at = pl.multiple_of(slot * RG * planes, RG * planes)
            row = pl.multiple_of(idx_ref[chunk * per_chunk + slot] * RG, RG)
            for j in range(turn_ref.shape[0]):
                cols = slice(j * LANES, (j + 1) * LANES)
                turn_ref[j] = got_ref[pl.ds(at, RG * planes), cols].astype(F32)
                for plane in range(planes):
                    value = turn_ref[j, pl.ds(plane, RG, stride=planes), :]
                    out_ref[plane, pl.ds(row, RG), cols] = value.astype(BF16)
            return carry

        here = jnp.clip(count - chunk * per_chunk, 0, per_chunk)
        lax.fori_loop(0, here, one, 0)


def per_device(g_upper, p_diag, p_upper, v_diag, v_upper, v_pattern, element_present):
    peers = lax.axis_size("energy")
    halves, local, _, size, _ = g_upper.shape
    planes = halves * local
    energies = local * peers
    chunks = CHUNKS
    rows = RG // chunks
    live = LIVE * RG
    flat = live * planes
    piece = flat // chunks

    green = g_upper.reshape(planes, size, size)
    p_d = p_diag.reshape(planes, size, size)
    p_u = p_upper.reshape(planes, size, size)
    v_d = v_diag.reshape(size, size)
    v_u = v_upper.reshape(size, size)
    present = element_present.reshape(-1)
    groups = present.shape[0]

    present_prev = shifted(present, 1)
    present_next = shifted(present, -1)
    v_u_prev = shifted(v_u, 1)
    v_d_next = shifted(v_d, -1)
    forward, inverse = tables(energies, peers)

    idx = pltpu.SMEM((groups,), jnp.int32)
    square = pltpu.VMEM((size, size), F32)
    strip = pltpu.VMEM((live, size), F32)
    total = pltpu.VMEM((size // LANES, flat, LANES), F32)
    turn = pltpu.VMEM((size // LANES, RG * planes, LANES), F32)

    def cost(units, data):
        return pl.CostEstimate(
            flops=int(units * 2 * planes * live * size * size), bytes_accessed=int(data), transcendentals=0
        )

    big = planes * size * size * 2

    send_green = pl.pallas_call(
        functools.partial(pack_kernel, chunks),
        out_shape=jax.ShapeDtypeStruct((peers, RG, planes, size), BF16),
        in_specs=[smem(), vmem()],
        out_specs=vmem(),
        scratch_shapes=[idx, turn],
        cost_estimate=cost(0.2, 2 * big),
        name="pack",
    )(present, green)
    got_green = lax.all_to_all(send_green, "energy", split_axis=0, concat_axis=0, tiled=True)

    to_next = pl.pallas_call(
        forward_kernel,
        out_shape=jax.ShapeDtypeStruct((flat, size), BF16),
        in_specs=[smem(), smem(), vmem(), vmem()],
        out_specs=vmem(),
        scratch_shapes=[idx, square, strip, total],
        cost_estimate=cost(1, 2 * big),
        name="to_next",
    )(present_next, v_pattern, v_u, p_u)
    to_prev = pl.pallas_call(
        backward_kernel,
        out_shape=jax.ShapeDtypeStruct((flat, size), BF16),
        in_specs=[smem(), smem()] + [vmem()] * 5,
        out_specs=vmem(),
        scratch_shapes=[idx, square, strip, total],
        cost_estimate=cost(4, 3 * big),
        name="to_prev",
    )(present_prev, v_pattern, v_u_prev, v_d, v_u, p_d, p_u)

    to_prev, v_d_next = lax.optimization_barrier((to_prev, v_d_next))
    before, after = [], []
    for chunk in range(chunks):
        part = slice(chunk * piece, (chunk + 1) * piece)
        before.append(shifted(to_next[part], 1))
        after.append(shifted(to_prev[part], -1))

    own = pl.pallas_call(
        local_kernel,
        out_shape=jax.ShapeDtypeStruct((flat, size), F32),
        in_specs=[smem(), smem()] + [vmem()] * 5,
        out_specs=vmem(),
        scratch_shapes=[idx, square, strip, strip, total, total, total],
        cost_estimate=cost(5, 4 * big),
        name="own",
    )(present, v_pattern, v_u, v_d, v_d_next, p_d, p_u)

    green_freq = pl.pallas_call(
        functools.partial(spectrum_kernel, 1.0 / (energies * math.sqrt(energies))),
        out_shape=jax.ShapeDtypeStruct((RG, 2 * energies, size), F32),
        in_specs=[vmem(), vmem()],
        out_specs=vmem(),
        cost_estimate=cost(0.5, 3 * big),
        name="green_freq",
    )(forward, got_green)

    returned = []
    for chunk in range(chunks):
        part = slice(chunk * piece, (chunk + 1) * piece)
        send = pl.pallas_call(
            join_kernel,
            out_shape=jax.ShapeDtypeStruct((peers * rows * planes, size), BF16),
            grid=(1,),
            in_specs=[
                smem(),
                pl.BlockSpec((piece, size), lambda i, c=chunk: (c, 0)),
                vmem(),
                vmem(),
                vmem(),
            ],
            out_specs=vmem(),
            cost_estimate=cost(1 / chunks, 3 * big / chunks),
            name="join",
        )(v_pattern, own, before[chunk], after[chunk], v_u)
        got = lax.all_to_all(
            send.reshape(peers, rows, planes, size), "energy", split_axis=0, concat_axis=0, tiled=True
        )
        result = pl.pallas_call(
            convolve_kernel,
            out_shape=jax.ShapeDtypeStruct((peers, rows, planes, size), BF16),
            grid=(1,),
            in_specs=[
                vmem(),
                vmem(),
                pl.BlockSpec((rows, 2 * energies, size), lambda i, c=chunk: (c, 0, 0)),
                vmem(),
            ],
            out_specs=vmem(),
            cost_estimate=cost(1 / chunks, 3 * big / chunks),
            name="convolve",
        )(forward, inverse, green_freq, got)
        back = lax.all_to_all(result, "energy", split_axis=0, concat_axis=0, tiled=True)
        returned.append(back.reshape(peers * rows * planes, size))

    sigma = pl.pallas_call(
        functools.partial(unpack_kernel, chunks),
        out_shape=jax.ShapeDtypeStruct((planes, size, size), BF16),
        in_specs=[smem()] + [vmem()] * chunks,
        out_specs=vmem(),
        scratch_shapes=[idx, turn],
        cost_estimate=cost(0.2, 2 * big),
        name="unpack",
    )(present, *returned)
    return sigma.reshape(halves, local, 1, size, size)


def solution(mesh):
    in_specs = (
        P(None, "energy", "space", None, None),
        P(None, "energy", "space", None, None),
        P(None, "energy", "space", None, None),
        P("space", None, None),
        P("space", None, None),
        P("space"),
        P("space", None),
    )
    out_specs = P(None, "energy", "space", None, None)
    return jax.shard_map(
        per_device, mesh=mesh, in_specs=in_specs, out_specs=out_specs, check_vma=False
    )
```

```python
import functools
import math

import jax
import jax.numpy as jnp
import numpy as np
from jax import lax
from jax.experimental import pallas as pl
from jax.experimental.pallas import tpu as pltpu
from jax.sharding import PartitionSpec as P


LIVE = 30
RG = 8
LANES = 128
ROWS = (8,)

F32 = jnp.float32
BF16 = jnp.bfloat16


def smem():
    return pl.BlockSpec(memory_space=pltpu.SMEM)


def vmem():
    return pl.BlockSpec(memory_space=pltpu.VMEM)


def hbm():
    return pl.BlockSpec(memory_space=pltpu.HBM)


def shifted(value, steps):
    count = lax.axis_size("space")
    pairs = [(source, (source + steps) % count) for source in range(count)]
    return lax.ppermute(value, "space", pairs)


def routed(value):
    return lax.all_to_all(value, "energy", split_axis=0, concat_axis=0, tiled=True)


def dot(left, right):
    return lax.dot_general(left, right, (((1,), (0,)), ((), ())), preferred_element_type=F32)


def dot_nt(left, right):
    return lax.dot_general(left, right, (((1,), (1,)), ((), ())), preferred_element_type=F32)


def tables(energies, peers):
    local = energies // peers
    src, half, step = np.meshgrid(np.arange(peers), np.arange(2), np.arange(local), indexing="ij")
    time = (src * local + step).reshape(-1)
    half = half.reshape(-1)
    freq = np.arange(energies)
    angles = 2.0 * math.pi / energies * ((freq[:, None] * time[None, :]) % energies)
    cosine, sine = np.cos(angles), np.sin(angles)
    real_part = np.where(half == 0, cosine, sine)
    imag_part = np.where(half == 0, -sine, cosine)
    forward = np.concatenate([real_part, imag_part], 0)
    real_out = np.concatenate([-sine, -cosine], 0).T
    imag_out = np.concatenate([cosine, -sine], 0).T
    inverse = np.where((half == 0)[:, None], real_out, imag_out)
    return jnp.asarray(forward, BF16), jnp.asarray(inverse, BF16)


def spread(dest_ref, plane, planes, value):
    rows = value.shape[0]
    for j in range(value.shape[1] // LANES):
        dest_ref[j, pl.ds(plane, rows, stride=planes), :] = value[:, j * LANES : (j + 1) * LANES]


def joined(source_ref):
    return jnp.concatenate([source_ref[j] for j in range(source_ref.shape[0])], axis=1)


def live_list(present_ref, idx_ref):
    for slot in range(LIVE):
        idx_ref[slot] = 0
    count = jnp.int32(0)
    for group in range(present_ref.shape[0]):
        idx_ref[count] = group
        count = count + jnp.where(present_ref[group] > 0, 1, 0)
    return count


def pick_rows(idx_ref, source_ref, dest_ref):
    for slot in range(LIVE):
        row = pl.multiple_of(idx_ref[slot] * RG, RG)
        dest_ref[slot * RG : (slot + 1) * RG, :] = source_ref[pl.ds(row, RG), :]


def place(row):
    start = 0
    for chunk, rows in enumerate(ROWS):
        if row < start + LIVE * rows:
            peer, inner = divmod(row - start, rows)
            return chunk, peer, inner
        start += LIVE * rows


def pieces(planes):
    starts = np.concatenate([[0], np.cumsum(ROWS)]) * LIVE * planes
    return [(int(x), int(y)) for x, y in zip(starts[:-1], starts[1:])]


def pack_kernel(present_ref, g_ref, out_ref, idx_ref, turn_ref, held_ref, sem):
    planes = g_ref.shape[0]
    live_list(present_ref, idx_ref)
    firsts = np.concatenate([[0], np.cumsum(ROWS)])
    copies = []
    for slot in range(LIVE):
        row = pl.multiple_of(idx_ref[slot] * RG, RG)
        copies.append(
            pltpu.make_async_copy(g_ref.at[:, pl.ds(row, RG), :], held_ref.at[slot], sem.at[slot])
        )
        copies[-1].start()
    for slot in range(LIVE):
        turn = turn_ref.at[slot % turn_ref.shape[0]]
        copies[slot].wait()
        for plane in range(planes):
            spread(turn, plane, planes, held_ref[slot, plane].astype(F32))
        value = joined(turn).astype(BF16)
        for r in range(RG):
            chunk, peer, inner = place(slot * RG + r)
            out_ref[peer, int(firsts[chunk]) + inner] = value[r * planes : (r + 1) * planes]
    for peer in range(LIVE, out_ref.shape[0]):
        out_ref[peer] = jnp.zeros(out_ref.shape[1:], BF16)


def inner_kernel(pattern_ref, vd_ref, vu_ref, pd_hbm, pu_hbm, out_ref, pu_ref, pd_ref, sem):
    planes = pu_ref.shape[0]
    copies = []
    for plane in range(planes):
        copies.append(
            (
                pltpu.make_async_copy(pd_hbm.at[plane], pd_ref.at[plane], sem.at[0, plane]),
                pltpu.make_async_copy(pu_hbm.at[plane], pu_ref.at[plane], sem.at[1, plane]),
            )
        )
        for copy in copies[-1]:
            copy.start()
    scale = pattern_ref[0].astype(F32)
    turned = ((vu_ref[...].astype(F32) * scale).T).astype(BF16)
    right = jnp.concatenate([vd_ref[...], turned], axis=0)
    for plane in range(planes):
        for copy in copies[plane]:
            copy.wait()
        left = jnp.concatenate([pd_ref[plane], pu_ref[plane]], axis=1)
        out_ref[plane] = dot(left, right).astype(BF16)


def outward_kernel(next_ref, prev_ref, pattern_ref, vu_ref, vu_prev_ref, pu_ref, inner_ref, *refs):
    chunks = len(ROWS)
    to_next, to_prev = refs[:chunks], refs[chunks : 2 * chunks]
    idx_next, idx_prev, wide, picked, total_next, total_prev = refs[2 * chunks :]
    planes = pu_ref.shape[0]
    live_list(prev_ref, idx_prev)
    live_list(next_ref, idx_next)
    wide[...] = vu_prev_ref[...].astype(F32)
    pick_rows(idx_prev, wide, picked)
    left_prev = picked[...].astype(BF16)
    scale = pattern_ref[0].astype(F32)
    wide[...] = (vu_ref[...].astype(F32) * scale).T
    pick_rows(idx_next, wide, picked)
    left_next = picked[...].astype(BF16)
    for plane in range(planes):
        spread(total_prev, plane, planes, dot(left_prev, inner_ref[plane]))
        spread(total_next, plane, planes, dot(left_next, pu_ref[plane]))
    for chunk, (start, end) in enumerate(pieces(planes)):
        to_next[chunk][...] = joined(total_next.at[:, start:end]).astype(BF16)
        to_prev[chunk][...] = joined(total_prev.at[:, start:end]).astype(BF16)


def local_kernel(present_ref, pattern_ref, vu_ref, vd_ref, vd_next_ref, pd_hbm, pu_hbm, *refs):
    chunks = len(ROWS)
    outs = refs[:chunks]
    idx_ref, wide, picked_u, picked_d, same, one_up, bare, pd_ref, pu_ref, sem = refs[chunks:]
    planes = pu_ref.shape[0]
    copies = []
    for plane in range(planes):
        copies.append(
            (
                pltpu.make_async_copy(pd_hbm.at[plane], pd_ref.at[plane], sem.at[0, plane]),
                pltpu.make_async_copy(pu_hbm.at[plane], pu_ref.at[plane], sem.at[1, plane]),
            )
        )
        for copy in copies[-1]:
            copy.start()
    live_list(present_ref, idx_ref)
    scale = pattern_ref[0].astype(F32)
    wide[...] = vu_ref[...].astype(F32) * scale
    masked = wide[...].astype(BF16)
    pick_rows(idx_ref, wide, picked_u)
    wide[...] = vd_ref[...].astype(F32)
    pick_rows(idx_ref, wide, picked_d)
    left_u = picked_u[...].astype(BF16)
    left_d = picked_d[...].astype(BF16)
    nothing = jnp.zeros(picked_u.shape, F32)
    for plane in range(planes):
        for copy in copies[plane]:
            copy.wait()
        spread(same, plane, planes, dot(left_d, pd_ref[plane]) + dot_nt(left_u, pu_ref[plane]))
        spread(one_up, plane, planes, dot(left_d, pu_ref[plane]))
        spread(bare, plane, planes, picked_u[...] if plane < planes // 2 else nothing)
    for out_ref, (start, end) in zip(outs, pieces(planes)):
        out_ref[...] = (
            joined(bare.at[:, start:end])
            + dot(joined(same.at[:, start:end]).astype(BF16), masked)
            + dot(joined(one_up.at[:, start:end]).astype(BF16), vd_next_ref[...])
        )


def join_kernel(pattern_ref, local_ref, before_ref, after_ref, vu_ref, out_ref):
    scale = pattern_ref[0].astype(F32)
    masked = (vu_ref[...].astype(F32) * scale).astype(BF16)
    size = local_ref.shape[0]
    out_ref[0:size, :] = (
        local_ref[...] + dot(before_ref[...], masked) + after_ref[...].astype(F32) * scale
    ).astype(BF16)
    out_ref[size:, :] = jnp.zeros((out_ref.shape[0] - size, out_ref.shape[1]), BF16)


def spectrum_kernel(scale, forward_ref, got_ref, *outs):
    peers, _, planes, cols = got_ref.shape
    at = 0
    for out_ref in outs:
        for r in range(out_ref.shape[0]):
            values = got_ref[:, at].reshape(peers * planes, cols)
            out_ref[r] = dot(forward_ref[...], values) * scale
            at += 1


def convolve_kernel(forward_ref, inverse_ref, green_ref, got_ref, out_ref):
    peers, rows, planes, cols = got_ref.shape
    half = forward_ref.shape[0] // 2
    for r in range(rows):
        values = got_ref[:, r].reshape(peers * planes, cols)
        freq = dot(forward_ref[...], values)
        green_re, green_im = green_ref[r, :half], green_ref[r, half:]
        screen_re, screen_im = freq[:half], freq[half:]
        mixed = jnp.concatenate(
            [green_re * screen_re - green_im * screen_im, green_re * screen_im + green_im * screen_re], 0
        )
        result = dot(inverse_ref[...], mixed.astype(BF16)).astype(BF16)
        out_ref[:, r] = result.reshape(peers, planes, cols)


def unpack_kernel(present_ref, *refs):
    chunks = len(ROWS)
    got_refs, (out_ref, idx_ref, turn_ref) = refs[:chunks], refs[chunks:]
    planes = out_ref.shape[0]
    count = live_list(present_ref, idx_ref)
    out_ref[...] = jnp.zeros(out_ref.shape, BF16)
    for slot in range(LIVE):

        @pl.when(slot < count)
        def _(slot=slot):
            turn = turn_ref.at[slot % turn_ref.shape[0]]
            row = pl.multiple_of(idx_ref[slot] * RG, RG)
            for r in range(RG):
                chunk, peer, inner = place(slot * RG + r)
                at = (peer * ROWS[chunk] + inner) * planes
                value = got_refs[chunk][at : at + planes, :].astype(F32)
                for j in range(turn.shape[0]):
                    turn[j, r * planes : (r + 1) * planes] = value[:, j * LANES : (j + 1) * LANES]
            for plane in range(planes):
                value = [turn[j, pl.ds(plane, RG, stride=planes), :] for j in range(turn.shape[0])]
                out_ref[plane, pl.ds(row, RG), :] = jnp.concatenate(value, 1).astype(BF16)


def per_device(g_upper, p_diag, p_upper, v_diag, v_upper, v_pattern, element_present):
    peers = lax.axis_size("energy")
    halves, local, _, size, _ = g_upper.shape
    planes = halves * local
    energies = local * peers
    live = LIVE * RG
    flat = live * planes
    sizes = [end - start for start, end in pieces(planes)]

    green = g_upper.reshape(planes, size, size)
    p_d = p_diag.reshape(planes, size, size)
    p_u = p_upper.reshape(planes, size, size)
    v_d = v_diag.reshape(size, size)
    v_u = v_upper.reshape(size, size)
    present = element_present.reshape(-1)
    groups = present.shape[0]

    present_prev = shifted(present, 1)
    present_next = shifted(present, -1)
    v_u_prev = shifted(v_u, 1)
    v_d_next = shifted(v_d, -1)
    forward, inverse = tables(energies, peers)

    idx = pltpu.SMEM((groups,), jnp.int32)
    square = pltpu.VMEM((size, size), F32)
    strip = pltpu.VMEM((live, size), F32)
    total = pltpu.VMEM((size // LANES, flat, LANES), F32)
    turn = pltpu.VMEM((4, size // LANES, RG * planes, LANES), F32)
    big = planes * size * size * 2

    def call(kernel, outs, ins, scratch, units, mib):
        many = isinstance(outs, list)
        return pl.pallas_call(
            kernel,
            out_shape=outs,
            in_specs=ins,
            out_specs=[vmem() for _ in outs] if many else vmem(),
            scratch_shapes=scratch,
            compiler_params=pltpu.CompilerParams(vmem_limit_bytes=mib * 2**20),
            cost_estimate=pl.CostEstimate(
                flops=int(units * 2 * planes * live * size * size), bytes_accessed=int(big), transcendentals=0
            ),
        )

    def array(*shape, dtype=BF16):
        return jax.ShapeDtypeStruct(shape, dtype)

    whole = pltpu.VMEM((planes, size, size), BF16)
    sems = pltpu.SemaphoreType.DMA((2, planes))
    inner, p_u_here = call(
        inner_kernel,
        [array(planes, size, size)] * 2,
        [smem()] + [vmem()] * 2 + [hbm()] * 2,
        [whole, sems],
        3.2,
        12,
    )(v_pattern, v_d, v_u, p_d, p_u)
    outward = call(
        outward_kernel,
        [array(n, size) for n in sizes] * 2,
        [smem()] * 3 + [vmem()] * 4,
        [idx, idx, square, strip, total, total],
        2,
        18,
    )(present_next, present_prev, v_pattern, v_u, v_u_prev, p_u_here, inner)
    chunks = len(ROWS)
    before = [shifted(piece, 1) for piece in outward[:chunks]]
    after = [shifted(piece, -1) for piece in outward[chunks:]]

    held = pltpu.VMEM((LIVE, planes, RG, size), BF16)
    held_sem = pltpu.SemaphoreType.DMA((LIVE,))
    send_green = call(
        pack_kernel, array(peers, RG, planes, size), [smem(), hbm()], [idx, turn, held, held_sem], 0.3, 8
    )(present, green)
    got_green = routed(send_green)

    own = call(
        local_kernel,
        [array(n, size, dtype=F32) for n in sizes],
        [smem()] * 2 + [vmem()] * 3 + [hbm()] * 2,
        [idx, square, strip, strip, total, total, total, whole, whole, sems],
        5,
        22,
    )(present, v_pattern, v_u, v_d, v_d_next, p_d, p_u)

    green_freq = call(
        functools.partial(spectrum_kernel, 1.0 / (energies * math.sqrt(energies))),
        [array(rows, 2 * energies, size, dtype=F32) for rows in ROWS],
        [vmem(), vmem()],
        [],
        0.5,
        8,
    )(forward, got_green)

    returned = []
    for chunk, rows in enumerate(ROWS):
        send = call(
            join_kernel,
            array(peers * rows * planes, size),
            [smem()] + [vmem()] * 4,
            [],
            rows / RG,
            8,
        )(v_pattern, own[chunk], before[chunk], after[chunk], v_u)
        got = routed(send.reshape(peers, rows, planes, size))
        result = call(
            convolve_kernel, array(peers, rows, planes, size), [vmem()] * 4, [], rows / RG, 10
        )(forward, inverse, green_freq[chunk], got)
        back = routed(result)
        returned.append(back.reshape(peers * rows * planes, size))

    sigma = call(
        unpack_kernel, array(planes, size, size), [smem()] + [vmem()] * chunks, [idx, turn], 0.3, 8
    )(present, *returned)
    return sigma.reshape(halves, local, 1, size, size)


def solution(mesh):
    in_specs = (
        P(None, "energy", "space", None, None),
        P(None, "energy", "space", None, None),
        P(None, "energy", "space", None, None),
        P("space", None, None),
        P("space", None, None),
        P("space"),
        P("space", None),
    )
    out_specs = P(None, "energy", "space", None, None)

    return jax.shard_map(per_device, mesh=mesh, in_specs=in_specs, out_specs=out_specs, check_vma=False)
```

```python
import functools
import math

import jax
import jax.numpy as jnp
import numpy as np
from jax import lax
from jax.experimental import pallas as pl
from jax.experimental.pallas import tpu as pltpu
from jax.sharding import PartitionSpec as P


LIVE = 30
RG = 8
LANES = 128
ROWS = (8,)

F32 = jnp.float32
BF16 = jnp.bfloat16


def smem():
    return pl.BlockSpec(memory_space=pltpu.SMEM)


def vmem():
    return pl.BlockSpec(memory_space=pltpu.VMEM)


def hbm():
    return pl.BlockSpec(memory_space=pltpu.HBM)


def shifted(value, steps):
    count = lax.axis_size("space")
    pairs = [(source, (source + steps) % count) for source in range(count)]
    return lax.ppermute(value, "space", pairs)


def routed(value):
    return lax.all_to_all(value, "energy", split_axis=0, concat_axis=0, tiled=True)


def dot(left, right):
    return lax.dot_general(left, right, (((1,), (0,)), ((), ())), preferred_element_type=F32)


def dot_nt(left, right):
    return lax.dot_general(left, right, (((1,), (1,)), ((), ())), preferred_element_type=F32)


def tables(energies, peers):
    local = energies // peers
    src, half, step = np.meshgrid(np.arange(peers), np.arange(2), np.arange(local), indexing="ij")
    time = (src * local + step).reshape(-1)
    half = half.reshape(-1)
    freq = np.arange(energies)
    angles = 2.0 * math.pi / energies * ((freq[:, None] * time[None, :]) % energies)
    cosine, sine = np.cos(angles), np.sin(angles)
    real_part = np.where(half == 0, cosine, sine)
    imag_part = np.where(half == 0, -sine, cosine)
    forward = np.concatenate([real_part, imag_part], 0)
    real_out = np.concatenate([-sine, -cosine], 0).T
    imag_out = np.concatenate([cosine, -sine], 0).T
    inverse = np.where((half == 0)[:, None], real_out, imag_out)
    return jnp.asarray(forward, BF16), jnp.asarray(inverse, BF16)


def fetch(sources, targets, sems):
    copies = [pltpu.make_async_copy(a, b, sem) for a, b, sem in zip(sources, targets, sems)]
    for copy in copies:
        copy.start()
    return copies


def arrive(copies):
    for copy in copies:
        copy.wait()


def spread(dest_ref, plane, planes, value):
    rows = value.shape[0]
    for j in range(value.shape[1] // LANES):
        dest_ref[j, pl.ds(plane, rows, stride=planes), :] = value[:, j * LANES : (j + 1) * LANES]


def joined(source_ref):
    return jnp.concatenate([source_ref[j] for j in range(source_ref.shape[0])], axis=1)


def live_list(present_ref, idx_ref):
    for slot in range(LIVE):
        idx_ref[slot] = 0
    count = jnp.int32(0)
    for group in range(present_ref.shape[0]):
        idx_ref[count] = group
        count = count + jnp.where(present_ref[group] > 0, 1, 0)
    return count


def pick_rows(idx_ref, source_ref, dest_ref):
    for slot in range(LIVE):
        row = pl.multiple_of(idx_ref[slot] * RG, RG)
        dest_ref[slot * RG : (slot + 1) * RG, :] = source_ref[pl.ds(row, RG), :]


def place(row):
    start = 0
    for chunk, rows in enumerate(ROWS):
        if row < start + LIVE * rows:
            peer, inner = divmod(row - start, rows)
            return chunk, peer, inner
        start += LIVE * rows


def pieces(planes):
    starts = np.concatenate([[0], np.cumsum(ROWS)]) * LIVE * planes
    return [(int(x), int(y)) for x, y in zip(starts[:-1], starts[1:])]


def pack_kernel(present_ref, g_ref, out_ref, idx_ref, turn_ref, held_ref, sem):
    planes = g_ref.shape[0]
    live_list(present_ref, idx_ref)
    firsts = np.concatenate([[0], np.cumsum(ROWS)])
    copies = []
    for slot in range(LIVE):
        row = pl.multiple_of(idx_ref[slot] * RG, RG)
        copies.append(
            pltpu.make_async_copy(g_ref.at[:, pl.ds(row, RG), :], held_ref.at[slot], sem.at[slot])
        )
        copies[-1].start()
    for slot in range(LIVE):
        turn = turn_ref.at[slot % turn_ref.shape[0]]
        copies[slot].wait()
        for plane in range(planes):
            spread(turn, plane, planes, held_ref[slot, plane].astype(F32))
        value = joined(turn).astype(BF16)
        for r in range(RG):
            chunk, peer, inner = place(slot * RG + r)
            out_ref[peer, int(firsts[chunk]) + inner] = value[r * planes : (r + 1) * planes]
    for peer in range(LIVE, out_ref.shape[0]):
        out_ref[peer] = jnp.zeros(out_ref.shape[1:], BF16)


def inner_kernel(
    pattern_ref, vd_hbm, vu_hbm, pd_hbm, pu_hbm, out_ref, pu_ref, pd_ref, vd_ref, vu_ref, sem, v_sem
):
    planes = pu_ref.shape[0]
    small = fetch([vd_hbm, vu_hbm], [vd_ref, vu_ref], [v_sem.at[0], v_sem.at[1]])
    copies = [
        fetch(
            [pd_hbm.at[plane], pu_hbm.at[plane]],
            [pd_ref.at[plane], pu_ref.at[plane]],
            [sem.at[0, plane], sem.at[1, plane]],
        )
        for plane in range(planes)
    ]
    arrive(small)
    scale = pattern_ref[0].astype(F32)
    turned = ((vu_ref[...].astype(F32) * scale).T).astype(BF16)
    right = jnp.concatenate([vd_ref[...], turned], axis=0)
    for plane in range(planes):
        arrive(copies[plane])
        left = jnp.concatenate([pd_ref[plane], pu_ref[plane]], axis=1)
        out_ref[plane] = dot(left, right).astype(BF16)


def outward_kernel(next_ref, prev_ref, pattern_ref, vu_hbm, vu_prev_ref, pu_ref, inner_ref, *refs):
    chunks = len(ROWS)
    to_next, to_prev = refs[:chunks], refs[chunks : 2 * chunks]
    idx_next, idx_prev, vu_ref, wide, picked, total, ready, v_sem, sem = refs[2 * chunks :]
    planes = pu_ref.shape[0]
    small = fetch([vu_hbm], [vu_ref], [v_sem.at[0]])
    scale = pattern_ref[0].astype(F32)
    live_list(prev_ref, idx_prev)
    wide[0] = vu_prev_ref[...].astype(F32)
    pick_rows(idx_prev, wide.at[0], picked.at[0])
    live_list(next_ref, idx_next)
    arrive(small)
    wide[1] = (vu_ref[...].astype(F32) * scale).T
    pick_rows(idx_next, wide.at[1], picked.at[1])
    copies = []
    for way, (right_ref, outs) in enumerate(((inner_ref, to_prev), (pu_ref, to_next))):
        left = picked[way].astype(BF16)
        for plane in range(planes):
            spread(total.at[way], plane, planes, dot(left, right_ref[plane]))
        for chunk, (start, end) in enumerate(pieces(planes)):
            ready[way, start:end] = joined(total.at[way, :, start:end]).astype(BF16)
            copies += fetch([ready.at[way, start:end]], [outs[chunk]], [sem.at[way, chunk]])
    arrive(copies)


def local_kernel(present_ref, pattern_ref, vu_hbm, vd_hbm, vd_next_ref, pd_hbm, pu_hbm, *refs):
    chunks = len(ROWS)
    outs = refs[:chunks]
    idx_ref, wide, picked_u, picked_d, same, one_up, bare, pd_ref, pu_ref, vd_ref, vu_ref, sem, v_sem = refs[
        chunks:
    ]
    planes = pu_ref.shape[0]
    small = fetch([vd_hbm, vu_hbm], [vd_ref, vu_ref], [v_sem.at[0], v_sem.at[1]])
    copies = [
        fetch(
            [pd_hbm.at[plane], pu_hbm.at[plane]],
            [pd_ref.at[plane], pu_ref.at[plane]],
            [sem.at[0, plane], sem.at[1, plane]],
        )
        for plane in range(planes)
    ]
    live_list(present_ref, idx_ref)
    arrive(small)
    scale = pattern_ref[0].astype(F32)
    wide[...] = vu_ref[...].astype(F32) * scale
    masked = wide[...].astype(BF16)
    pick_rows(idx_ref, wide, picked_u)
    wide[...] = vd_ref[...].astype(F32)
    pick_rows(idx_ref, wide, picked_d)
    left_u = picked_u[...].astype(BF16)
    left_d = picked_d[...].astype(BF16)
    nothing = jnp.zeros(picked_u.shape, F32)
    for plane in range(planes):
        arrive(copies[plane])
        spread(same, plane, planes, dot(left_d, pd_ref[plane]) + dot_nt(left_u, pu_ref[plane]))
        spread(one_up, plane, planes, dot(left_d, pu_ref[plane]))
        spread(bare, plane, planes, picked_u[...] if plane < planes // 2 else nothing)
    for out_ref, (start, end) in zip(outs, pieces(planes)):
        out_ref[...] = (
            joined(bare.at[:, start:end])
            + dot(joined(same.at[:, start:end]).astype(BF16), masked)
            + dot(joined(one_up.at[:, start:end]).astype(BF16), vd_next_ref[...])
        )


def join_kernel(pattern_ref, local_ref, before_hbm, after_hbm, vu_hbm, out_ref, before, after, vu_ref, sem, v_sem):
    scale = pattern_ref[0].astype(F32)
    size = local_ref.shape[0]
    parts = sem.shape[1]
    step = size // parts
    small = fetch([vu_hbm], [vu_ref], [v_sem.at[0]])
    copies = []
    for part in range(parts):
        rows = slice(part * step, (part + 1) * step)
        copies.append(
            fetch(
                [before_hbm.at[rows], after_hbm.at[rows]],
                [before.at[rows], after.at[rows]],
                [sem.at[0, part], sem.at[1, part]],
            )
        )
    out_ref[size:, :] = jnp.zeros((out_ref.shape[0] - size, out_ref.shape[1]), BF16)
    arrive(small)
    masked = (vu_ref[...].astype(F32) * scale).astype(BF16)
    for part in range(parts):
        rows = slice(part * step, (part + 1) * step)
        arrive(copies[part])
        out_ref[rows, :] = (
            local_ref[rows, :] + dot(before[rows], masked) + after[rows].astype(F32) * scale
        ).astype(BF16)


def spectrum_kernel(scale, forward_ref, got_ref, *outs):
    peers, _, planes, cols = got_ref.shape
    at = 0
    for out_ref in outs:
        for r in range(out_ref.shape[0]):
            values = got_ref[:, at].reshape(peers * planes, cols)
            out_ref[r] = dot(forward_ref[...], values) * scale
            at += 1


def convolve_kernel(forward_ref, inverse_ref, green_ref, got_ref, out_ref):
    peers, rows, planes, cols = got_ref.shape
    half = forward_ref.shape[0] // 2
    for r in range(rows):
        values = got_ref[:, r].reshape(peers * planes, cols)
        freq = dot(forward_ref[...], values)
        green_re, green_im = green_ref[r, :half], green_ref[r, half:]
        screen_re, screen_im = freq[:half], freq[half:]
        mixed = jnp.concatenate(
            [green_re * screen_re - green_im * screen_im, green_re * screen_im + green_im * screen_re], 0
        )
        result = dot(inverse_ref[...], mixed.astype(BF16)).astype(BF16)
        out_ref[:, r] = result.reshape(peers, planes, cols)


def unpack_kernel(present_ref, *refs):
    chunks = len(ROWS)
    got_refs, (out_hbm, idx_ref, rest_ref, turn_ref, ready, nothing, sem) = refs[:chunks], refs[chunks:]
    groups = present_ref.shape[0]
    planes = out_hbm.shape[0]
    nothing[...] = jnp.zeros(nothing.shape, BF16)
    for slot in range(LIVE):
        idx_ref[slot] = 0
    count = jnp.int32(0)
    for group in range(groups):
        live = jnp.where(present_ref[group] > 0, 1, 0)
        idx_ref[count] = group
        rest_ref[group - count] = group
        count = count + live

    def out_rows(group):
        return out_hbm.at[:, pl.ds(pl.multiple_of(group * RG, RG), RG), :]

    def blank(at):
        group = rest_ref[at]
        return pltpu.make_async_copy(nothing, out_rows(group), sem.at[group])

    def start_blank(at, carry):
        blank(at).start()
        return carry

    def wait_blank(at, carry):
        blank(at).wait()
        return carry

    lax.fori_loop(0, groups - count, start_blank, 0)
    for slot in range(LIVE):

        @pl.when(slot < count)
        def _(slot=slot):
            turn = turn_ref.at[slot % turn_ref.shape[0]]
            group = idx_ref[slot]
            for r in range(RG):
                chunk, peer, inner = place(slot * RG + r)
                at = (peer * ROWS[chunk] + inner) * planes
                value = got_refs[chunk][at : at + planes, :].astype(F32)
                for j in range(turn.shape[0]):
                    turn[j, r * planes : (r + 1) * planes] = value[:, j * LANES : (j + 1) * LANES]
            for plane in range(planes):
                value = [turn[j, pl.ds(plane, RG, stride=planes), :] for j in range(turn.shape[0])]
                ready[slot, plane] = jnp.concatenate(value, 1).astype(BF16)
            pltpu.make_async_copy(ready.at[slot], out_rows(group), sem.at[group]).start()

    def wait_live(slot, carry):
        group = idx_ref[slot]
        pltpu.make_async_copy(ready.at[slot], out_rows(group), sem.at[group]).wait()
        return carry

    lax.fori_loop(0, count, wait_live, 0)
    lax.fori_loop(0, groups - count, wait_blank, 0)


def per_device(g_upper, p_diag, p_upper, v_diag, v_upper, v_pattern, element_present):
    peers = lax.axis_size("energy")
    halves, local, _, size, _ = g_upper.shape
    planes = halves * local
    energies = local * peers
    live = LIVE * RG
    flat = live * planes
    sizes = [end - start for start, end in pieces(planes)]

    def stay(value):
        return pltpu.with_memory_space_constraint(value, pltpu.HBM)

    green, p_d, p_u = (stay(x.reshape(planes, size, size)) for x in (g_upper, p_diag, p_upper))
    v_d, v_u = (x.reshape(size, size) for x in (v_diag, v_upper))
    v_d_here, v_u_here = stay(v_d), stay(v_u)
    present = element_present.reshape(-1)
    groups = present.shape[0]

    present_prev = shifted(present, 1)
    present_next = shifted(present, -1)
    v_u_prev = shifted(v_u, 1)
    v_d_next = shifted(v_d, -1)
    forward, inverse = tables(energies, peers)

    idx = pltpu.SMEM((groups,), jnp.int32)
    square = pltpu.VMEM((size, size), F32)
    strip = pltpu.VMEM((live, size), F32)
    total = pltpu.VMEM((size // LANES, flat, LANES), F32)
    turn = pltpu.VMEM((4, size // LANES, RG * planes, LANES), F32)
    big = planes * size * size * 2

    def call(kernel, outs, ins, scratch, units, mib, place_out=vmem):
        many = isinstance(outs, list)
        return pl.pallas_call(
            kernel,
            out_shape=outs,
            in_specs=ins,
            out_specs=[place_out() for _ in outs] if many else place_out(),
            scratch_shapes=scratch,
            compiler_params=pltpu.CompilerParams(vmem_limit_bytes=mib * 2**20),
            cost_estimate=pl.CostEstimate(
                flops=int(units * 2 * planes * live * size * size), bytes_accessed=int(big), transcendentals=0
            ),
        )

    def array(*shape, dtype=BF16):
        return jax.ShapeDtypeStruct(shape, dtype)

    whole = pltpu.VMEM((planes, size, size), BF16)
    sems = pltpu.SemaphoreType.DMA((2, planes))
    pair = pltpu.SemaphoreType.DMA((2,))
    block = pltpu.VMEM((size, size), BF16)
    inner, p_u_held = call(
        inner_kernel,
        [array(planes, size, size)] * 2,
        [smem()] + [hbm()] * 4,
        [whole, block, block, sems, pair],
        3.2,
        12,
    )(v_pattern, v_d_here, v_u_here, p_d, p_u)
    outward = call(
        outward_kernel,
        [array(n, size) for n in sizes] * 2,
        [smem()] * 3 + [hbm()] + [vmem()] * 3,
        [
            idx,
            idx,
            block,
            pltpu.VMEM((2, size, size), F32),
            pltpu.VMEM((2, live, size), F32),
            pltpu.VMEM((2, size // LANES, flat, LANES), F32),
            pltpu.VMEM((2, flat, size), BF16),
            pair,
            pltpu.SemaphoreType.DMA((2, len(ROWS))),
        ],
        2,
        20,
        hbm,
    )(present_next, present_prev, v_pattern, v_u_here, v_u_prev, p_u_held, inner)
    chunks = len(ROWS)
    before = [shifted(piece, 1) for piece in outward[:chunks]]
    after = [shifted(piece, -1) for piece in outward[chunks:]]

    held = pltpu.VMEM((LIVE, planes, RG, size), BF16)
    held_sem = pltpu.SemaphoreType.DMA((LIVE,))
    send_green = call(
        pack_kernel, array(peers, RG, planes, size), [smem(), hbm()], [idx, turn, held, held_sem], 0.3, 8
    )(present, green)
    got_green = routed(send_green)

    own = call(
        local_kernel,
        [array(n, size, dtype=F32) for n in sizes],
        [smem()] * 2 + [hbm()] * 2 + [vmem()] + [hbm()] * 2,
        [idx, square, strip, strip, total, total, total, whole, whole, block, block, sems, pair],
        5,
        22,
    )(present, v_pattern, v_u_here, v_d_here, v_d_next, p_d, p_u)

    green_freq = call(
        functools.partial(spectrum_kernel, 1.0 / (energies * math.sqrt(energies))),
        [array(rows, 2 * energies, size, dtype=F32) for rows in ROWS],
        [vmem(), vmem()],
        [],
        0.5,
        8,
    )(forward, got_green)

    returned = []
    for chunk, rows in enumerate(ROWS):
        send = call(
            join_kernel,
            array(peers * rows * planes, size),
            [smem(), vmem()] + [hbm()] * 3,
            [
                pltpu.VMEM((sizes[chunk], size), BF16),
                pltpu.VMEM((sizes[chunk], size), BF16),
                block,
                pltpu.SemaphoreType.DMA((2, 5)),
                pair,
            ],
            rows / RG,
            10,
        )(v_pattern, own[chunk], stay(before[chunk]), stay(after[chunk]), v_u_here)
        got = routed(send.reshape(peers, rows, planes, size))
        result = call(
            convolve_kernel, array(peers, rows, planes, size), [vmem()] * 4, [], rows / RG, 10
        )(forward, inverse, green_freq[chunk], got)
        back = routed(result)
        returned.append(back.reshape(peers * rows * planes, size))

    sigma = call(
        unpack_kernel,
        array(planes, size, size),
        [smem()] + [vmem()] * chunks,
        [
            idx,
            idx,
            turn,
            held,
            pltpu.VMEM((planes, RG, size), BF16),
            pltpu.SemaphoreType.DMA((groups,)),
        ],
        0.3,
        8,
        hbm,
    )(present, *returned)
    return sigma.reshape(halves, local, 1, size, size)


def solution(mesh):
    in_specs = (
        P(None, "energy", "space", None, None),
        P(None, "energy", "space", None, None),
        P(None, "energy", "space", None, None),
        P("space", None, None),
        P("space", None, None),
        P("space"),
        P("space", None),
    )
    out_specs = P(None, "energy", "space", None, None)

    return jax.shard_map(per_device, mesh=mesh, in_specs=in_specs, out_specs=out_specs, check_vma=False)
```

```python
import functools
import math

import jax
import jax.numpy as jnp
import numpy as np
from jax import lax
from jax.experimental import pallas as pl
from jax.experimental.pallas import tpu as pltpu
from jax.sharding import PartitionSpec as P


LIVE = 30
RG = 8
LANES = 128
ROWS = (8,)
PARTS = (0, 120, 240)

F32 = jnp.float32
BF16 = jnp.bfloat16


def smem():
    return pl.BlockSpec(memory_space=pltpu.SMEM)


def vmem():
    return pl.BlockSpec(memory_space=pltpu.VMEM)


def hbm():
    return pl.BlockSpec(memory_space=pltpu.HBM)


def shifted(value, steps):
    count = lax.axis_size("space")
    pairs = [(source, (source + steps) % count) for source in range(count)]
    return lax.ppermute(value, "space", pairs)


def routed(value):
    return lax.all_to_all(value, "energy", split_axis=0, concat_axis=0, tiled=True)


def dot(left, right):
    return lax.dot_general(left, right, (((1,), (0,)), ((), ())), preferred_element_type=F32)


def dot_nt(left, right):
    return lax.dot_general(left, right, (((1,), (1,)), ((), ())), preferred_element_type=F32)


def tables(energies, peers):
    local = energies // peers
    src, half, step = np.meshgrid(np.arange(peers), np.arange(2), np.arange(local), indexing="ij")
    time = (src * local + step).reshape(-1)
    half = half.reshape(-1)
    freq = np.arange(energies)
    angles = 2.0 * math.pi / energies * ((freq[:, None] * time[None, :]) % energies)
    cosine, sine = np.cos(angles), np.sin(angles)
    real_part = np.where(half == 0, cosine, sine)
    imag_part = np.where(half == 0, -sine, cosine)
    forward = np.concatenate([real_part, imag_part], 0)
    real_out = np.concatenate([-sine, -cosine], 0).T
    imag_out = np.concatenate([cosine, -sine], 0).T
    inverse = np.where((half == 0)[:, None], real_out, imag_out)
    return jnp.asarray(forward, BF16), jnp.asarray(inverse, BF16)


def fetch(sources, targets, sems):
    copies = [pltpu.make_async_copy(a, b, sem) for a, b, sem in zip(sources, targets, sems)]
    for copy in copies:
        copy.start()
    return copies


def arrive(copies):
    for copy in copies:
        copy.wait()


def spread(dest_ref, plane, planes, value):
    rows = value.shape[0]
    for j in range(value.shape[1] // LANES):
        dest_ref[j, pl.ds(plane, rows, stride=planes), :] = value[:, j * LANES : (j + 1) * LANES]


def joined(source_ref):
    return jnp.concatenate([source_ref[j] for j in range(source_ref.shape[0])], axis=1)


def live_list(present_ref, idx_ref):
    for slot in range(LIVE):
        idx_ref[slot] = 0
    count = jnp.int32(0)
    for group in range(present_ref.shape[0]):
        idx_ref[count] = group
        count = count + jnp.where(present_ref[group] > 0, 1, 0)
    return count


def pick_rows(idx_ref, source_ref, dest_ref):
    for slot in range(LIVE):
        row = pl.multiple_of(idx_ref[slot] * RG, RG)
        dest_ref[slot * RG : (slot + 1) * RG, :] = source_ref[pl.ds(row, RG), :]


def place(row):
    start = 0
    for chunk, rows in enumerate(ROWS):
        if row < start + LIVE * rows:
            peer, inner = divmod(row - start, rows)
            return chunk, peer, inner
        start += LIVE * rows


def pack_kernel(present_ref, g_ref, out_ref, idx_ref, turn_ref, held_ref, sem):
    planes = g_ref.shape[0]
    live_list(present_ref, idx_ref)
    firsts = np.concatenate([[0], np.cumsum(ROWS)])
    copies = []
    for slot in range(LIVE):
        row = pl.multiple_of(idx_ref[slot] * RG, RG)
        copies.append(
            pltpu.make_async_copy(g_ref.at[:, pl.ds(row, RG), :], held_ref.at[slot], sem.at[slot])
        )
        copies[-1].start()
    for slot in range(LIVE):
        turn = turn_ref.at[slot % turn_ref.shape[0]]
        copies[slot].wait()
        for plane in range(planes):
            spread(turn, plane, planes, held_ref[slot, plane].astype(F32))
        value = joined(turn).astype(BF16)
        for r in range(RG):
            chunk, peer, inner = place(slot * RG + r)
            out_ref[peer, int(firsts[chunk]) + inner] = value[r * planes : (r + 1) * planes]
    for peer in range(LIVE, out_ref.shape[0]):
        out_ref[peer] = jnp.zeros(out_ref.shape[1:], BF16)


def inner_kernel(pattern_ref, vd_ref, vu_ref, pd_ref, pu_ref, out_ref):
    scale = pattern_ref[0].astype(F32)
    turned = ((vu_ref[...].astype(F32) * scale).T).astype(BF16)
    right = jnp.concatenate([vd_ref[...], turned], axis=0)
    for plane in range(pu_ref.shape[0]):
        left = jnp.concatenate([pd_ref[plane], pu_ref[plane]], axis=1)
        out_ref[plane] = dot(left, right).astype(BF16)


def prepare_kernel(present_ref, pattern_ref, vu_ref, out_ref, idx_ref, wide, picked):
    live_list(present_ref, idx_ref)
    wide[...] = vu_ref[...].astype(F32) * pattern_ref[0].astype(F32)
    pick_rows(idx_ref, wide, picked)
    out_ref[...] = picked[...].astype(BF16)


def outward_kernel(next_ref, pattern_ref, vu_ref, left_ref, pu_ref, inner_ref, *refs):
    chunks = len(PARTS) - 1
    to_next, to_prev = refs[:chunks], refs[chunks : 2 * chunks]
    idx_next, wide, picked, total_next, total_prev = refs[2 * chunks :]
    planes = pu_ref.shape[0]
    live_list(next_ref, idx_next)
    wide[...] = (vu_ref[...].astype(F32) * pattern_ref[0].astype(F32)).T
    pick_rows(idx_next, wide, picked)
    left_next = picked[...].astype(BF16)
    left_prev = left_ref[...]
    for plane in range(planes):
        spread(total_prev, plane, planes, dot(left_prev, inner_ref[plane]))
        spread(total_next, plane, planes, dot(left_next, pu_ref[plane]))
    for chunk in range(chunks):
        rows = slice(PARTS[chunk] * planes, PARTS[chunk + 1] * planes)
        to_next[chunk][...] = joined(total_next.at[:, rows]).astype(BF16)
        to_prev[chunk][...] = joined(total_prev.at[:, rows]).astype(BF16)


def local_kernel(present_ref, pattern_ref, vu_hbm, vd_hbm, vd_next_ref, pd_hbm, pu_hbm, *refs):
    outs = refs[: len(PARTS) - 1]
    idx_ref, wide, picked_u, picked_d, same, one_up, bare, pd_ref, pu_ref, vd_ref, vu_ref, sem, v_sem = refs[
        len(outs) :
    ]
    planes = pu_ref.shape[0]
    small = fetch([vd_hbm, vu_hbm], [vd_ref, vu_ref], [v_sem.at[0], v_sem.at[1]])
    copies = [
        fetch(
            [pd_hbm.at[plane], pu_hbm.at[plane]],
            [pd_ref.at[plane], pu_ref.at[plane]],
            [sem.at[0, plane], sem.at[1, plane]],
        )
        for plane in range(planes)
    ]
    live_list(present_ref, idx_ref)
    arrive(small)
    scale = pattern_ref[0].astype(F32)
    wide[...] = vu_ref[...].astype(F32) * scale
    masked = wide[...].astype(BF16)
    pick_rows(idx_ref, wide, picked_u)
    wide[...] = vd_ref[...].astype(F32)
    pick_rows(idx_ref, wide, picked_d)
    left_u = picked_u[...].astype(BF16)
    left_d = picked_d[...].astype(BF16)
    nothing = jnp.zeros(picked_u.shape, F32)
    for plane in range(planes):
        arrive(copies[plane])
        spread(same, plane, planes, dot(left_d, pd_ref[plane]) + dot_nt(left_u, pu_ref[plane]))
        spread(one_up, plane, planes, dot(left_d, pu_ref[plane]))
        spread(bare, plane, planes, picked_u[...] if plane < planes // 2 else nothing)
    for part, out_ref in enumerate(outs):
        start, end = PARTS[part] * planes, PARTS[part + 1] * planes
        out_ref[...] = (
            joined(bare.at[:, start:end])
            + dot(joined(same.at[:, start:end]).astype(BF16), masked)
            + dot(joined(one_up.at[:, start:end]).astype(BF16), vd_next_ref[...])
        )


def join_kernel(part, pattern_ref, local_ref, before_hbm, after_hbm, vu_hbm, *refs):
    done_ref = refs[0] if part else None
    out_ref, before, after, vu_ref, sem, v_sem = refs[1 if part else 0 :]
    scale = pattern_ref[0].astype(F32)
    size = local_ref.shape[0]
    parts = sem.shape[1]
    step = size // parts
    small = fetch([vu_hbm], [vu_ref], [v_sem.at[0]])
    copies = []
    for at in range(parts):
        rows = slice(at * step, (at + 1) * step)
        copies.append(
            fetch(
                [before_hbm.at[rows], after_hbm.at[rows]],
                [before.at[rows], after.at[rows]],
                [sem.at[0, at], sem.at[1, at]],
            )
        )
    first = 0
    if part:
        first = done_ref.shape[0]
        out_ref[:first, :] = done_ref[...]
        tail = out_ref.shape[0] - first - size
        out_ref[first + size :, :] = jnp.zeros((tail, out_ref.shape[1]), BF16)
    arrive(small)
    masked = (vu_ref[...].astype(F32) * scale).astype(BF16)
    for at in range(parts):
        rows = slice(at * step, (at + 1) * step)
        arrive(copies[at])
        out_ref[first + at * step : first + (at + 1) * step, :] = (
            local_ref[rows, :] + dot(before[rows], masked) + after[rows].astype(F32) * scale
        ).astype(BF16)


def spectrum_kernel(scale, forward_ref, got_ref, *outs):
    peers, _, planes, cols = got_ref.shape
    at = 0
    for out_ref in outs:
        for r in range(out_ref.shape[0]):
            values = got_ref[:, at].reshape(peers * planes, cols)
            out_ref[r] = dot(forward_ref[...], values) * scale
            at += 1


def convolve_kernel(forward_ref, inverse_ref, green_ref, got_ref, out_ref):
    peers, rows, planes, cols = got_ref.shape
    half = forward_ref.shape[0] // 2
    for r in range(rows):
        values = got_ref[:, r].reshape(peers * planes, cols)
        freq = dot(forward_ref[...], values)
        green_re, green_im = green_ref[r, :half], green_ref[r, half:]
        screen_re, screen_im = freq[:half], freq[half:]
        mixed = jnp.concatenate(
            [green_re * screen_re - green_im * screen_im, green_re * screen_im + green_im * screen_re], 0
        )
        result = dot(inverse_ref[...], mixed.astype(BF16)).astype(BF16)
        out_ref[:, r] = result.reshape(peers, planes, cols)


def unpack_kernel(present_ref, *refs):
    chunks = len(ROWS)
    got_refs, (out_hbm, idx_ref, rest_ref, turn_ref, ready, nothing, sem) = refs[:chunks], refs[chunks:]
    groups = present_ref.shape[0]
    planes = out_hbm.shape[0]
    nothing[...] = jnp.zeros(nothing.shape, BF16)
    for slot in range(LIVE):
        idx_ref[slot] = 0
    count = jnp.int32(0)
    for group in range(groups):
        live = jnp.where(present_ref[group] > 0, 1, 0)
        idx_ref[count] = group
        rest_ref[group - count] = group
        count = count + live

    def out_rows(group):
        return out_hbm.at[:, pl.ds(pl.multiple_of(group * RG, RG), RG), :]

    def blank(at):
        group = rest_ref[at]
        return pltpu.make_async_copy(nothing, out_rows(group), sem.at[group])

    def start_blank(at, carry):
        blank(at).start()
        return carry

    def wait_blank(at, carry):
        blank(at).wait()
        return carry

    lax.fori_loop(0, groups - count, start_blank, 0)
    for slot in range(LIVE):

        @pl.when(slot < count)
        def _(slot=slot):
            turn = turn_ref.at[slot % turn_ref.shape[0]]
            group = idx_ref[slot]
            for r in range(RG):
                chunk, peer, inner = place(slot * RG + r)
                at = (peer * ROWS[chunk] + inner) * planes
                value = got_refs[chunk][at : at + planes, :].astype(F32)
                for j in range(turn.shape[0]):
                    turn[j, r * planes : (r + 1) * planes] = value[:, j * LANES : (j + 1) * LANES]
            for plane in range(planes):
                value = [turn[j, pl.ds(plane, RG, stride=planes), :] for j in range(turn.shape[0])]
                ready[slot, plane] = jnp.concatenate(value, 1).astype(BF16)
            pltpu.make_async_copy(ready.at[slot], out_rows(group), sem.at[group]).start()

    def wait_live(slot, carry):
        group = idx_ref[slot]
        pltpu.make_async_copy(ready.at[slot], out_rows(group), sem.at[group]).wait()
        return carry

    lax.fori_loop(0, count, wait_live, 0)
    lax.fori_loop(0, groups - count, wait_blank, 0)


def per_device(g_upper, p_diag, p_upper, v_diag, v_upper, v_pattern, element_present):
    peers = lax.axis_size("energy")
    halves, local, _, size, _ = g_upper.shape
    planes = halves * local
    energies = local * peers
    live = LIVE * RG
    flat = live * planes
    sizes = [(end - start) * planes for start, end in zip(PARTS[:-1], PARTS[1:])]

    def stay(value):
        return pltpu.with_memory_space_constraint(value, pltpu.HBM)

    green, p_d, p_u = (stay(x.reshape(planes, size, size)) for x in (g_upper, p_diag, p_upper))
    v_d, v_u = (x.reshape(size, size) for x in (v_diag, v_upper))
    v_d_here, v_u_here = stay(v_d), stay(v_u)

    def near(value):
        return pltpu.with_memory_space_constraint(value, pltpu.VMEM)

    p_d_near, p_u_near = near(p_diag.reshape(planes, size, size)), near(p_upper.reshape(planes, size, size))
    v_d_near, v_u_near = near(v_d), near(v_u)
    present = element_present.reshape(-1)
    groups = present.shape[0]

    idx = pltpu.SMEM((groups,), jnp.int32)
    square = pltpu.VMEM((size, size), F32)
    strip = pltpu.VMEM((live, size), F32)
    total = pltpu.VMEM((size // LANES, flat, LANES), F32)
    turn = pltpu.VMEM((4, size // LANES, RG * planes, LANES), F32)
    big = planes * size * size * 2

    def call(kernel, outs, ins, scratch, units, mib, place_out=vmem):
        many = isinstance(outs, list)
        return pl.pallas_call(
            kernel,
            out_shape=outs,
            in_specs=ins,
            out_specs=[place_out() for _ in outs] if many else place_out(),
            scratch_shapes=scratch,
            compiler_params=pltpu.CompilerParams(vmem_limit_bytes=mib * 2**20),
            cost_estimate=pl.CostEstimate(
                flops=int(units * 2 * planes * live * size * size), bytes_accessed=int(big), transcendentals=0
            ),
        )

    def array(*shape, dtype=BF16):
        return jax.ShapeDtypeStruct(shape, dtype)

    chosen = call(
        prepare_kernel, array(live, size), [smem()] * 2 + [vmem()], [idx, square, strip], 8, 6
    )(present, v_pattern, v_u)
    present_next = shifted(present, -1)
    v_u_prev = shifted(chosen, 1)
    v_d_next = shifted(v_d, -1)
    forward, inverse = tables(energies, peers)

    whole = pltpu.VMEM((planes, size, size), BF16)
    sems = pltpu.SemaphoreType.DMA((2, planes))
    pair = pltpu.SemaphoreType.DMA((2,))
    block = pltpu.VMEM((size, size), BF16)
    inner = call(
        inner_kernel, array(planes, size, size), [smem()] + [vmem()] * 4, [], 3.2, 12
    )(v_pattern, v_d_near, v_u_near, p_d_near, p_u_near)
    outward = call(
        outward_kernel,
        [array(n, size) for n in sizes] * 2,
        [smem()] * 2 + [vmem()] * 4,
        [idx, square, strip, total, total],
        2,
        18,
    )(present_next, v_pattern, v_u_near, v_u_prev, p_u_near, inner)
    chunks = len(sizes)
    before = [shifted(piece, 1) for piece in outward[:chunks]]
    after = [shifted(piece, -1) for piece in outward[chunks:]]

    held = pltpu.VMEM((LIVE, planes, RG, size), BF16)
    held_sem = pltpu.SemaphoreType.DMA((LIVE,))
    send_green = call(
        pack_kernel, array(peers, RG, planes, size), [smem(), hbm()], [idx, turn, held, held_sem], 0.3, 8
    )(present, green)
    got_green = routed(send_green)

    own = call(
        local_kernel,
        [array(n, size, dtype=F32) for n in sizes],
        [smem()] * 2 + [hbm()] * 2 + [vmem()] + [hbm()] * 2,
        [idx, square, strip, strip, total, total, total, whole, whole, block, block, sems, pair],
        5,
        22,
    )(present, v_pattern, v_u_here, v_d_here, v_d_next, p_d, p_u)

    green_freq = call(
        functools.partial(spectrum_kernel, 1.0 / (energies * math.sqrt(energies))),
        [array(rows, 2 * energies, size, dtype=F32) for rows in ROWS],
        [vmem(), vmem()],
        [],
        0.5,
        8,
    )(forward, got_green)

    joined_parts = []
    for part, rows in enumerate(sizes):
        last = part == len(sizes) - 1
        joined_parts.append(
            call(
                functools.partial(join_kernel, part),
                array(peers * RG * planes if last else rows, size),
                [smem(), vmem()] + [hbm()] * 3 + [vmem()] * part,
                [
                    pltpu.VMEM((rows, size), BF16),
                    pltpu.VMEM((rows, size), BF16),
                    block,
                    pltpu.SemaphoreType.DMA((2, 3)),
                    pair,
                ],
                0.5,
                8,
            )(v_pattern, own[part], stay(before[part]), stay(after[part]), v_u_here, *joined_parts)
        )
    got = routed(joined_parts[-1].reshape(peers, RG, planes, size))
    result = call(
        convolve_kernel, array(peers, RG, planes, size), [vmem()] * 4, [], 1, 10
    )(forward, inverse, green_freq[0], got)
    returned = [routed(result).reshape(peers * RG * planes, size)]

    sigma = call(
        unpack_kernel,
        array(planes, size, size),
        [smem()] + [vmem()] * len(returned),
        [
            idx,
            idx,
            turn,
            held,
            pltpu.VMEM((planes, RG, size), BF16),
            pltpu.SemaphoreType.DMA((groups,)),
        ],
        0.3,
        8,
        hbm,
    )(present, *returned)
    return sigma.reshape(halves, local, 1, size, size)


def solution(mesh):
    in_specs = (
        P(None, "energy", "space", None, None),
        P(None, "energy", "space", None, None),
        P(None, "energy", "space", None, None),
        P("space", None, None),
        P("space", None, None),
        P("space"),
        P("space", None),
    )
    out_specs = P(None, "energy", "space", None, None)

    return jax.shard_map(per_device, mesh=mesh, in_specs=in_specs, out_specs=out_specs, check_vma=False)
```

```python
import functools
import math

import jax
import jax.numpy as jnp
import numpy as np
from jax import lax
from jax.experimental import pallas as pl
from jax.experimental.pallas import tpu as pltpu
from jax.sharding import PartitionSpec as P


LIVE = 30
RG = 8
LANES = 128
ROWS = (8,)

F32 = jnp.float32
BF16 = jnp.bfloat16


def smem():
    return pl.BlockSpec(memory_space=pltpu.SMEM)


def vmem():
    return pl.BlockSpec(memory_space=pltpu.VMEM)


def hbm():
    return pl.BlockSpec(memory_space=pltpu.HBM)


def shifted(value, steps):
    count = lax.axis_size("space")
    pairs = [(source, (source + steps) % count) for source in range(count)]
    return lax.ppermute(value, "space", pairs)


def routed(value):
    return lax.all_to_all(value, "energy", split_axis=0, concat_axis=0, tiled=True)


def dot(left, right):
    return lax.dot_general(left, right, (((1,), (0,)), ((), ())), preferred_element_type=F32)


def dot_nt(left, right):
    return lax.dot_general(left, right, (((1,), (1,)), ((), ())), preferred_element_type=F32)


def tables(energies, peers):
    local = energies // peers
    src, half, step = np.meshgrid(np.arange(peers), np.arange(2), np.arange(local), indexing="ij")
    time = (src * local + step).reshape(-1)
    half = half.reshape(-1)
    freq = np.arange(energies)
    angles = 2.0 * math.pi / energies * ((freq[:, None] * time[None, :]) % energies)
    cosine, sine = np.cos(angles), np.sin(angles)
    real_part = np.where(half == 0, cosine, sine)
    imag_part = np.where(half == 0, -sine, cosine)
    forward = np.concatenate([real_part, imag_part], 0)
    real_out = np.concatenate([-sine, -cosine], 0).T
    imag_out = np.concatenate([cosine, -sine], 0).T
    inverse = np.where((half == 0)[:, None], real_out, imag_out)
    return jnp.asarray(forward, BF16), jnp.asarray(inverse, BF16)


def fetch(sources, targets, sems):
    copies = [pltpu.make_async_copy(a, b, sem) for a, b, sem in zip(sources, targets, sems)]
    for copy in copies:
        copy.start()
    return copies


def arrive(copies):
    for copy in copies:
        copy.wait()


def spread(dest_ref, plane, planes, value):
    rows = value.shape[0]
    for j in range(value.shape[1] // LANES):
        dest_ref[j, pl.ds(plane, rows, stride=planes), :] = value[:, j * LANES : (j + 1) * LANES]


def joined(source_ref):
    return jnp.concatenate([source_ref[j] for j in range(source_ref.shape[0])], axis=1)


def live_list(present_ref, idx_ref):
    for slot in range(LIVE):
        idx_ref[slot] = 0
    count = jnp.int32(0)
    for group in range(present_ref.shape[0]):
        idx_ref[count] = group
        count = count + jnp.where(present_ref[group] > 0, 1, 0)
    return count


def pick_rows(idx_ref, source_ref, dest_ref):
    for slot in range(LIVE):
        row = pl.multiple_of(idx_ref[slot] * RG, RG)
        dest_ref[slot * RG : (slot + 1) * RG, :] = source_ref[pl.ds(row, RG), :]


def place(row):
    start = 0
    for chunk, rows in enumerate(ROWS):
        if row < start + LIVE * rows:
            peer, inner = divmod(row - start, rows)
            return chunk, peer, inner
        start += LIVE * rows


def pack_kernel(present_ref, g_ref, out_ref, idx_ref, turn_ref):
    planes = g_ref.shape[0]
    live_list(present_ref, idx_ref)
    firsts = np.concatenate([[0], np.cumsum(ROWS)])
    for slot in range(LIVE):
        turn = turn_ref.at[slot % turn_ref.shape[0]]
        row = pl.multiple_of(idx_ref[slot] * RG, RG)
        for plane in range(planes):
            spread(turn, plane, planes, g_ref[plane, pl.ds(row, RG), :].astype(F32))
        value = joined(turn).astype(BF16)
        for r in range(RG):
            chunk, peer, inner = place(slot * RG + r)
            out_ref[peer, int(firsts[chunk]) + inner] = value[r * planes : (r + 1) * planes]
    for peer in range(LIVE, out_ref.shape[0]):
        out_ref[peer] = jnp.zeros(out_ref.shape[1:], BF16)


def inner_kernel(pattern_ref, vd_ref, vu_ref, pd_ref, pu_ref, out_ref):
    scale = pattern_ref[0].astype(F32)
    turned = ((vu_ref[...].astype(F32) * scale).T).astype(BF16)
    right = jnp.concatenate([vd_ref[...], turned], axis=0)
    for plane in range(pu_ref.shape[0]):
        left = jnp.concatenate([pd_ref[plane], pu_ref[plane]], axis=1)
        out_ref[plane] = dot(left, right).astype(BF16)


def prepare_kernel(present_ref, pattern_ref, vu_ref, out_ref, idx_ref, wide, picked):
    live_list(present_ref, idx_ref)
    wide[...] = vu_ref[...].astype(F32) * pattern_ref[0].astype(F32)
    pick_rows(idx_ref, wide, picked)
    out_ref[...] = picked[...].astype(BF16)


def outward_kernel(
    next_ref, pattern_ref, vu_ref, left_ref, pu_ref, inner_ref, to_next, to_prev, idx, wide, picked, ready, sem
):
    planes = pu_ref.shape[0]
    live_list(next_ref, idx)
    wide[...] = (vu_ref[...].astype(F32) * pattern_ref[0].astype(F32)).T
    pick_rows(idx, wide, picked)
    left_next = picked[...].astype(BF16)
    left_prev = left_ref[...]
    copies = []
    for plane in range(planes):
        ready[0, plane] = dot(left_prev, inner_ref[plane]).astype(BF16)
        copies += fetch([ready.at[0, plane]], [to_prev.at[plane]], [sem.at[0, plane]])
        ready[1, plane] = dot(left_next, pu_ref[plane]).astype(BF16)
        copies += fetch([ready.at[1, plane]], [to_next.at[plane]], [sem.at[1, plane]])
    arrive(copies)


def local_kernel(
    present_ref,
    pattern_ref,
    vu_hbm,
    vd_hbm,
    vd_next_ref,
    pd_hbm,
    pu_hbm,
    out_ref,
    idx_ref,
    wide,
    picked_u,
    picked_d,
    same,
    one_up,
    pd_ref,
    pu_ref,
    vd_ref,
    vu_ref,
    sem,
    v_sem,
):
    planes = pu_ref.shape[0]
    rows = LIVE * RG
    small = fetch([vd_hbm, vu_hbm], [vd_ref, vu_ref], [v_sem.at[0], v_sem.at[1]])
    copies = [
        fetch(
            [pd_hbm.at[plane], pu_hbm.at[plane]],
            [pd_ref.at[plane], pu_ref.at[plane]],
            [sem.at[0, plane], sem.at[1, plane]],
        )
        for plane in range(planes)
    ]
    live_list(present_ref, idx_ref)
    arrive(small)
    wide[...] = vu_ref[...].astype(F32) * pattern_ref[0].astype(F32)
    masked = wide[...].astype(BF16)
    pick_rows(idx_ref, wide, picked_u)
    wide[...] = vd_ref[...].astype(F32)
    pick_rows(idx_ref, wide, picked_d)
    left_u = picked_u[...].astype(BF16)
    left_d = picked_d[...].astype(BF16)
    for plane in range(planes):
        arrive(copies[plane])
        at = slice(plane * rows, (plane + 1) * rows)
        same[at] = (dot(left_d, pd_ref[plane]) + dot_nt(left_u, pu_ref[plane])).astype(BF16)
        one_up[at] = dot(left_d, pu_ref[plane]).astype(BF16)
    for plane in range(planes):
        at = slice(plane * rows, (plane + 1) * rows)
        value = dot(same[at], masked) + dot(one_up[at], vd_next_ref[...])
        if plane < planes // 2:
            value = value + picked_u[...]
        out_ref[plane] = value.astype(BF16)


def join_kernel(pattern_ref, local_ref, before_hbm, after_hbm, vu_hbm, out_ref, before, after, vu_ref, total, sem, v_sem):
    planes, rows, cols = local_ref.shape
    size = planes * rows
    scale = pattern_ref[0].astype(F32)
    small = fetch([vu_hbm], [vu_ref], [v_sem.at[0]])
    copies = [
        fetch(
            [before_hbm.at[plane], after_hbm.at[plane]],
            [before.at[plane], after.at[plane]],
            [sem.at[0, plane], sem.at[1, plane]],
        )
        for plane in range(planes)
    ]
    out_ref[size:, :] = jnp.zeros((out_ref.shape[0] - size, cols), BF16)
    arrive(small)
    masked = (vu_ref[...].astype(F32) * scale).astype(BF16)
    for plane in range(planes):
        arrive(copies[plane])
        value = dot(before[plane], masked) + after[plane].astype(F32) * scale
        spread(total, plane, planes, value + local_ref[plane].astype(F32))
    out_ref[:size, :] = joined(total).astype(BF16)


def spectrum_kernel(scale, forward_ref, got_ref, *outs):
    peers, _, planes, cols = got_ref.shape
    at = 0
    for out_ref in outs:
        for r in range(out_ref.shape[0]):
            values = got_ref[:, at].reshape(peers * planes, cols)
            out_ref[r] = dot(forward_ref[...], values) * scale
            at += 1


def convolve_kernel(forward_ref, inverse_ref, green_ref, got_ref, out_ref):
    peers, rows, planes, cols = got_ref.shape
    half = forward_ref.shape[0] // 2
    for r in range(rows):
        values = got_ref[:, r].reshape(peers * planes, cols)
        freq = dot(forward_ref[...], values)
        green_re, green_im = green_ref[r, :half], green_ref[r, half:]
        screen_re, screen_im = freq[:half], freq[half:]
        mixed = jnp.concatenate(
            [green_re * screen_re - green_im * screen_im, green_re * screen_im + green_im * screen_re], 0
        )
        result = dot(inverse_ref[...], mixed.astype(BF16)).astype(BF16)
        out_ref[:, r] = result.reshape(peers, planes, cols)


def unpack_kernel(present_ref, *refs):
    chunks = len(ROWS)
    got_refs, (out_hbm, idx_ref, rest_ref, turn_ref, ready, nothing, sem) = refs[:chunks], refs[chunks:]
    groups = present_ref.shape[0]
    planes = out_hbm.shape[0]
    nothing[...] = jnp.zeros(nothing.shape, BF16)
    for slot in range(LIVE):
        idx_ref[slot] = 0
    count = jnp.int32(0)
    for group in range(groups):
        live = jnp.where(present_ref[group] > 0, 1, 0)
        idx_ref[count] = group
        rest_ref[group - count] = group
        count = count + live

    def out_rows(group):
        return out_hbm.at[:, pl.ds(pl.multiple_of(group * RG, RG), RG), :]

    def blank(at):
        group = rest_ref[at]
        return pltpu.make_async_copy(nothing, out_rows(group), sem.at[group])

    def start_blank(at, carry):
        blank(at).start()
        return carry

    def wait_blank(at, carry):
        blank(at).wait()
        return carry

    lax.fori_loop(0, groups - count, start_blank, 0)
    for slot in range(LIVE):

        @pl.when(slot < count)
        def _(slot=slot):
            turn = turn_ref.at[slot % turn_ref.shape[0]]
            group = idx_ref[slot]
            for r in range(RG):
                chunk, peer, inner = place(slot * RG + r)
                at = (peer * ROWS[chunk] + inner) * planes
                value = got_refs[chunk][at : at + planes, :].astype(F32)
                for j in range(turn.shape[0]):
                    turn[j, r * planes : (r + 1) * planes] = value[:, j * LANES : (j + 1) * LANES]
            for plane in range(planes):
                value = [turn[j, pl.ds(plane, RG, stride=planes), :] for j in range(turn.shape[0])]
                ready[slot, plane] = jnp.concatenate(value, 1).astype(BF16)
            pltpu.make_async_copy(ready.at[slot], out_rows(group), sem.at[group]).start()

    def wait_live(slot, carry):
        group = idx_ref[slot]
        pltpu.make_async_copy(ready.at[slot], out_rows(group), sem.at[group]).wait()
        return carry

    lax.fori_loop(0, count, wait_live, 0)
    lax.fori_loop(0, groups - count, wait_blank, 0)


def per_device(g_upper, p_diag, p_upper, v_diag, v_upper, v_pattern, element_present):
    peers = lax.axis_size("energy")
    halves, local, _, size, _ = g_upper.shape
    planes = halves * local
    energies = local * peers
    live = LIVE * RG
    flat = live * planes

    def stay(value):
        return pltpu.with_memory_space_constraint(value, pltpu.HBM)

    p_d, p_u = (stay(x.reshape(planes, size, size)) for x in (p_diag, p_upper))
    v_d, v_u = (x.reshape(size, size) for x in (v_diag, v_upper))
    v_d_here, v_u_here = stay(v_d), stay(v_u)

    def near(value):
        return pltpu.with_memory_space_constraint(value, pltpu.VMEM)

    p_d_near, p_u_near, green = (
        near(x.reshape(planes, size, size)) for x in (p_diag, p_upper, g_upper)
    )
    v_d_near, v_u_near = near(v_d), near(v_u)
    present = element_present.reshape(-1)
    groups = present.shape[0]

    idx = pltpu.SMEM((groups,), jnp.int32)
    square = pltpu.VMEM((size, size), F32)
    strip = pltpu.VMEM((live, size), F32)
    total = pltpu.VMEM((size // LANES, flat, LANES), F32)
    turn = pltpu.VMEM((4, size // LANES, RG * planes, LANES), F32)
    big = planes * size * size * 2

    def call(kernel, outs, ins, scratch, units, mib, place_out=vmem):
        many = isinstance(outs, list)
        return pl.pallas_call(
            kernel,
            out_shape=outs,
            in_specs=ins,
            out_specs=[place_out() for _ in outs] if many else place_out(),
            scratch_shapes=scratch,
            compiler_params=pltpu.CompilerParams(vmem_limit_bytes=mib * 2**20),
            cost_estimate=pl.CostEstimate(
                flops=int(units * 2 * planes * live * size * size), bytes_accessed=int(big), transcendentals=0
            ),
        )

    def array(*shape, dtype=BF16):
        return jax.ShapeDtypeStruct(shape, dtype)

    chosen = call(
        prepare_kernel, array(live, size), [smem()] * 2 + [vmem()], [idx, square, strip], 8, 6
    )(present, v_pattern, v_u)
    present_next = shifted(present, -1)
    v_u_prev = shifted(chosen, 1)
    v_d_next = shifted(v_d, -1)
    forward, inverse = tables(energies, peers)

    whole = pltpu.VMEM((planes, size, size), BF16)
    sems = pltpu.SemaphoreType.DMA((2, planes))
    pair = pltpu.SemaphoreType.DMA((2,))
    block = pltpu.VMEM((size, size), BF16)
    inner = call(
        inner_kernel, array(planes, size, size), [smem()] + [vmem()] * 4, [], 3.2, 12
    )(v_pattern, v_d_near, v_u_near, p_d_near, p_u_near)
    parcel = pltpu.VMEM((planes, live, size), BF16)
    to_next, to_prev = call(
        outward_kernel,
        [array(planes, live, size)] * 2,
        [smem()] * 2 + [vmem()] * 4,
        [idx, square, strip, pltpu.VMEM((2, planes, live, size), BF16), sems],
        2,
        10,
        hbm,
    )(present_next, v_pattern, v_u_near, v_u_prev, p_u_near, inner)
    after = shifted(to_prev, -1)
    before = shifted(to_next, 1)

    held = pltpu.VMEM((LIVE, planes, RG, size), BF16)
    send_green = call(
        pack_kernel, array(peers, RG, planes, size), [smem(), vmem()], [idx, turn], 0.3, 8
    )(present, green)
    got_green = routed(send_green)

    stacked = pltpu.VMEM((flat, size), BF16)
    own = call(
        local_kernel,
        array(planes, live, size),
        [smem()] * 2 + [hbm()] * 2 + [vmem()] + [hbm()] * 2,
        [idx, square, strip, strip, stacked, stacked, whole, whole, block, block, sems, pair],
        5,
        16,
    )(present, v_pattern, v_u_here, v_d_here, v_d_next, p_d, p_u)

    green_freq = call(
        functools.partial(spectrum_kernel, 1.0 / (energies * math.sqrt(energies))),
        [array(rows, 2 * energies, size, dtype=F32) for rows in ROWS],
        [vmem(), vmem()],
        [],
        0.5,
        8,
    )(forward, got_green)

    send = call(
        join_kernel,
        array(peers * RG * planes, size),
        [smem(), vmem()] + [hbm()] * 3,
        [parcel, parcel, block, total, sems, pair],
        1,
        12,
    )(v_pattern, own, stay(before), stay(after), v_u_here)
    got = routed(send.reshape(peers, RG, planes, size))
    result = call(
        convolve_kernel, array(peers, RG, planes, size), [vmem()] * 4, [], 1, 10
    )(forward, inverse, green_freq[0], got)
    returned = [routed(result).reshape(peers * RG * planes, size)]

    sigma = call(
        unpack_kernel,
        array(planes, size, size),
        [smem()] + [vmem()] * len(returned),
        [
            idx,
            idx,
            turn,
            held,
            pltpu.VMEM((planes, RG, size), BF16),
            pltpu.SemaphoreType.DMA((groups,)),
        ],
        0.3,
        8,
        hbm,
    )(present, *returned)
    return sigma.reshape(halves, local, 1, size, size)


def solution(mesh):
    in_specs = (
        P(None, "energy", "space", None, None),
        P(None, "energy", "space", None, None),
        P(None, "energy", "space", None, None),
        P("space", None, None),
        P("space", None, None),
        P("space"),
        P("space", None),
    )
    out_specs = P(None, "energy", "space", None, None)

    return jax.shard_map(per_device, mesh=mesh, in_specs=in_specs, out_specs=out_specs, check_vma=False)
```

```python
import functools
import math

import jax
import jax.numpy as jnp
import numpy as np
from jax import lax
from jax.experimental import pallas as pl
from jax.experimental.pallas import tpu as pltpu
from jax.sharding import PartitionSpec as P


LIVE = 30
RG = 8
LANES = 128

F32 = jnp.float32
BF16 = jnp.bfloat16


def smem():
    return pl.BlockSpec(memory_space=pltpu.SMEM)


def vmem():
    return pl.BlockSpec(memory_space=pltpu.VMEM)


def hbm():
    return pl.BlockSpec(memory_space=pltpu.HBM)


def shifted(value, steps):
    count = lax.axis_size("space")
    pairs = [(source, (source + steps) % count) for source in range(count)]
    return lax.ppermute(value, "space", pairs)


def routed(value):
    return lax.all_to_all(value, "energy", split_axis=0, concat_axis=0, tiled=True)


def dot(left, right):
    return lax.dot_general(left, right, (((1,), (0,)), ((), ())), preferred_element_type=F32)


def dot_nt(left, right):
    return lax.dot_general(left, right, (((1,), (1,)), ((), ())), preferred_element_type=F32)


def tables(energies, peers):
    local = energies // peers
    src, half, step = np.meshgrid(np.arange(peers), np.arange(2), np.arange(local), indexing="ij")
    time = (src * local + step).reshape(-1)
    half = half.reshape(-1)
    freq = np.arange(energies)
    angles = 2.0 * math.pi / energies * ((freq[:, None] * time[None, :]) % energies)
    cosine, sine = np.cos(angles), np.sin(angles)
    real_part = np.where(half == 0, cosine, sine)
    imag_part = np.where(half == 0, -sine, cosine)
    forward = np.concatenate([real_part, imag_part], 0)
    real_out = np.concatenate([-sine, -cosine], 0).T
    imag_out = np.concatenate([cosine, -sine], 0).T
    inverse = np.where((half == 0)[:, None], real_out, imag_out)
    return jnp.asarray(forward, BF16), jnp.asarray(inverse, BF16)


def fetch(sources, targets, sems):
    copies = [pltpu.make_async_copy(a, b, sem) for a, b, sem in zip(sources, targets, sems)]
    for copy in copies:
        copy.start()
    return copies


def arrive(copies):
    for copy in copies:
        copy.wait()


def spread(dest_ref, plane, planes, value):
    rows = value.shape[0]
    for j in range(value.shape[1] // LANES):
        dest_ref[j, pl.ds(plane, rows, stride=planes), :] = value[:, j * LANES : (j + 1) * LANES]


def live_list(present_ref, idx_ref):
    for slot in range(LIVE):
        idx_ref[slot] = 0
    count = jnp.int32(0)
    for group in range(present_ref.shape[0]):
        idx_ref[count] = group
        count = count + jnp.where(present_ref[group] > 0, 1, 0)
    return count


def pick_rows(idx_ref, source_ref, dest_ref):
    for slot in range(LIVE):
        row = pl.multiple_of(idx_ref[slot] * RG, RG)
        dest_ref[slot * RG : (slot + 1) * RG, :] = source_ref[pl.ds(row, RG), :]


def pack_kernel(present_ref, g_ref, out_hbm, idx_ref, turn_ref, ready, sem):
    planes = g_ref.shape[0]
    tiles = g_ref.shape[2] // LANES
    span = LIVE * RG * planes
    live_list(present_ref, idx_ref)
    copies = []
    for tile in range(tiles):
        cols = slice(tile * LANES, (tile + 1) * LANES)
        for slot in range(LIVE):
            turn = turn_ref.at[slot % turn_ref.shape[0]]
            row = pl.multiple_of(idx_ref[slot] * RG, RG)
            for plane in range(planes):
                turn[pl.ds(plane, RG, stride=planes), :] = g_ref[plane, pl.ds(row, RG), cols].astype(F32)
            at = tile * span + slot * RG * planes
            ready[at : at + RG * planes, :] = turn[...].astype(BF16)
        end = (tile + 1) * span
        if tile == tiles - 1:
            ready[end:, :] = jnp.zeros((ready.shape[0] - end, LANES), BF16)
            end = ready.shape[0]
        rows = slice(tile * span, end)
        copies += fetch([ready.at[rows]], [out_hbm.at[rows]], [sem.at[tile]])
    arrive(copies)


def inner_kernel(pattern_ref, vd_ref, vu_ref, pd_ref, pu_ref, out_ref, turned_ref):
    scale = pattern_ref[0].astype(F32)
    turned = (vu_ref[...].astype(F32) * scale).T
    turned_ref[...] = turned
    right = jnp.concatenate([vd_ref[...], turned.astype(BF16)], axis=0)
    for plane in range(pu_ref.shape[0]):
        left = jnp.concatenate([pd_ref[plane], pu_ref[plane]], axis=1)
        out_ref[plane] = dot(left, right).astype(BF16)


def prepare_kernel(present_ref, pattern_ref, vu_ref, out_ref, idx_ref, wide, picked):
    live_list(present_ref, idx_ref)
    wide[...] = vu_ref[...].astype(F32) * pattern_ref[0].astype(F32)
    pick_rows(idx_ref, wide, picked)
    out_ref[...] = picked[...].astype(BF16)


def outward_kernel(next_ref, turned_ref, left_ref, pu_ref, inner_ref, to_next, to_prev, idx, picked, ready, sem):
    planes = pu_ref.shape[0]
    group = planes // sem.shape[1]
    left_prev = left_ref[...]
    copies = []
    for way, (right_ref, out_hbm) in enumerate(((inner_ref, to_prev), (pu_ref, to_next))):
        left = left_prev
        if way == 1:
            live_list(next_ref, idx)
            pick_rows(idx, turned_ref, picked)
            left = picked[...].astype(BF16)
        for plane in range(planes):
            ready[way, plane] = dot(left, right_ref[plane]).astype(BF16)
            if plane % group == group - 1:
                some = slice(plane + 1 - group, plane + 1)
                at = sem.at[way, plane // group]
                copies += fetch([ready.at[way, some]], [out_hbm.at[some]], [at])
    arrive(copies)


def local_kernel(
    present_ref,
    pattern_ref,
    vu_hbm,
    vd_hbm,
    vd_next_ref,
    pd_hbm,
    pu_hbm,
    out_ref,
    idx_ref,
    wide,
    picked_u,
    picked_d,
    same,
    one_up,
    pd_ref,
    pu_ref,
    vd_ref,
    vu_ref,
    sem,
    v_sem,
):
    planes = pu_ref.shape[0]
    rows = LIVE * RG
    small = fetch([vd_hbm, vu_hbm], [vd_ref, vu_ref], [v_sem.at[0], v_sem.at[1]])
    copies = [
        fetch(
            [pd_hbm.at[plane], pu_hbm.at[plane]],
            [pd_ref.at[plane], pu_ref.at[plane]],
            [sem.at[0, plane], sem.at[1, plane]],
        )
        for plane in range(planes)
    ]
    live_list(present_ref, idx_ref)
    arrive(small)
    wide[...] = vu_ref[...].astype(F32) * pattern_ref[0].astype(F32)
    masked = wide[...].astype(BF16)
    pick_rows(idx_ref, wide, picked_u)
    wide[...] = vd_ref[...].astype(F32)
    pick_rows(idx_ref, wide, picked_d)
    left_u = picked_u[...].astype(BF16)
    left_d = picked_d[...].astype(BF16)
    for plane in range(planes):
        arrive(copies[plane])
        at = slice(plane * rows, (plane + 1) * rows)
        same[at] = (dot(left_d, pd_ref[plane]) + dot_nt(left_u, pu_ref[plane])).astype(BF16)
        one_up[at] = dot(left_d, pu_ref[plane]).astype(BF16)
    for plane in range(planes):
        at = slice(plane * rows, (plane + 1) * rows)
        value = dot(same[at], masked) + dot(one_up[at], vd_next_ref[...])
        if plane < planes // 2:
            value = value + picked_u[...]
        out_ref[plane] = value.astype(BF16)


def join_kernel(pattern_ref, local_ref, before_hbm, after_hbm, vu_hbm, out_ref, before, after, vu_ref, total, sem, v_sem):
    planes, rows, cols = local_ref.shape
    parts = sem.shape[1]
    group = planes // parts
    scale = pattern_ref[0].astype(F32)
    small = fetch([vu_hbm], [vu_ref], [v_sem.at[0]])
    copies = []
    for part in range(parts):
        some = slice(part * group, (part + 1) * group)
        copies.append(
            fetch(
                [before_hbm.at[some], after_hbm.at[some]],
                [before.at[some], after.at[some]],
                [sem.at[0, part], sem.at[1, part]],
            )
        )
    size = total.shape[0] * total.shape[1]
    out_ref[size:, :] = jnp.zeros((out_ref.shape[0] - size, LANES), BF16)
    arrive(small)
    masked = (vu_ref[...].astype(F32) * scale).astype(BF16)
    for part in range(parts):
        some = slice(part * group, (part + 1) * group)
        arrive(copies[part])
        value = dot(before[some].reshape(group * rows, cols), masked)
        for inner in range(group):
            plane = part * group + inner
            rest = after[plane].astype(F32) * scale + local_ref[plane].astype(F32)
            spread(total, plane, planes, value[inner * rows : (inner + 1) * rows] + rest)
    for tile in range(total.shape[0]):
        at = slice(tile * total.shape[1], (tile + 1) * total.shape[1])
        out_ref[at, :] = total[tile].astype(BF16)


def unit_pairs(got_ref):
    peers, units, planes, lanes = got_ref.shape
    for first in range(0, units, 2):
        some = range(first, min(first + 2, units))
        yield first, [got_ref[:, unit].reshape(peers * planes, lanes) for unit in some]


def spectrum_kernel(scale, forward_ref, got_ref, out_ref):
    for first, values in unit_pairs(got_ref):
        width = LANES * len(values)
        out_ref[first // 2, :, :width] = dot(forward_ref[...], jnp.concatenate(values, 1)) * scale


def convolve_kernel(forward_ref, inverse_ref, green_ref, got_ref, out_ref):
    peers, _, planes, lanes = got_ref.shape
    half = forward_ref.shape[0] // 2
    for first, values in unit_pairs(got_ref):
        width = LANES * len(values)
        freq = dot(forward_ref[...], jnp.concatenate(values, 1))
        green_re, green_im = green_ref[first // 2, :half, :width], green_ref[first // 2, half:, :width]
        screen_re, screen_im = freq[:half], freq[half:]
        mixed = jnp.concatenate(
            [green_re * screen_re - green_im * screen_im, green_re * screen_im + green_im * screen_re], 0
        )
        result = dot(inverse_ref[...], mixed.astype(BF16)).astype(BF16)
        for at in range(len(values)):
            out_ref[:, first + at] = result[:, at * lanes : (at + 1) * lanes].reshape(peers, planes, lanes)


def unpack_kernel(present_ref, got_ref, out_hbm, turn_ref, ready, sem):
    groups = present_ref.shape[0]
    planes, _, cols = ready.shape
    tiles = cols // LANES
    span = LIVE * RG * planes
    batch = groups // sem.shape[0]
    copies = []
    slot = jnp.int32(0)
    for group in range(groups):
        rows = slice(group * RG, (group + 1) * RG)

        @pl.when(present_ref[group] > 0)
        def _(slot=slot, rows=rows):
            for tile in range(tiles):
                turn = turn_ref.at[tile]
                at = pl.multiple_of(tile * span + slot * RG * planes, RG * planes)
                turn[...] = got_ref[pl.ds(at, RG * planes), :].astype(F32)
                for plane in range(planes):
                    value = turn[pl.ds(plane, RG, stride=planes), :]
                    ready[plane, rows, tile * LANES : (tile + 1) * LANES] = value.astype(BF16)

        @pl.when(present_ref[group] <= 0)
        def _(rows=rows):
            ready[:, rows, :] = jnp.zeros((planes, RG, cols), BF16)

        slot = slot + jnp.where(present_ref[group] > 0, 1, 0)
        if group % batch == batch - 1:
            some = slice((group + 1 - batch) * RG, (group + 1) * RG)
            copies += fetch([ready.at[:, some]], [out_hbm.at[:, some]], [sem.at[group // batch]])
    arrive(copies)


def per_device(g_upper, p_diag, p_upper, v_diag, v_upper, v_pattern, element_present):
    peers = lax.axis_size("energy")
    halves, local, _, size, _ = g_upper.shape
    planes = halves * local
    energies = local * peers
    live = LIVE * RG
    flat = live * planes

    def stay(value):
        return pltpu.with_memory_space_constraint(value, pltpu.HBM)

    p_d, p_u = (stay(x.reshape(planes, size, size)) for x in (p_diag, p_upper))
    v_d, v_u = (x.reshape(size, size) for x in (v_diag, v_upper))
    v_d_here, v_u_here = stay(v_d), stay(v_u)

    def near(value):
        return pltpu.with_memory_space_constraint(value, pltpu.VMEM)

    p_d_near, p_u_near, green = (
        near(x.reshape(planes, size, size)) for x in (p_diag, p_upper, g_upper)
    )
    v_d_near, v_u_near = near(v_d), near(v_u)
    present = element_present.reshape(-1)
    groups = present.shape[0]
    tiles = size // LANES
    units = -(-live * tiles // peers)
    routes = peers * units * planes

    idx = pltpu.SMEM((groups,), jnp.int32)
    square = pltpu.VMEM((size, size), F32)
    strip = pltpu.VMEM((live, size), F32)
    total = pltpu.VMEM((size // LANES, flat, LANES), F32)
    turn = pltpu.VMEM((6, RG * planes, LANES), F32)
    big = planes * size * size * 2

    def call(kernel, outs, ins, scratch, units, mib, place_out=vmem):
        many = isinstance(outs, list)
        return pl.pallas_call(
            kernel,
            out_shape=outs,
            in_specs=ins,
            out_specs=[place_out() for _ in outs] if many else place_out(),
            scratch_shapes=scratch,
            compiler_params=pltpu.CompilerParams(vmem_limit_bytes=mib * 2**20),
            cost_estimate=pl.CostEstimate(
                flops=int(units * 2 * planes * live * size * size), bytes_accessed=int(big), transcendentals=0
            ),
        )

    def array(*shape, dtype=BF16):
        return jax.ShapeDtypeStruct(shape, dtype)

    chosen = call(
        prepare_kernel, array(live, size), [smem()] * 2 + [vmem()], [idx, square, strip], 8, 6
    )(present, v_pattern, v_u)
    v_u_prev = shifted(chosen, 1)
    present_next = shifted(present, -1)
    v_d_next = shifted(v_d, -1)
    forward, inverse = tables(energies, peers)

    whole = pltpu.VMEM((planes, size, size), BF16)
    sems = pltpu.SemaphoreType.DMA((2, planes))
    pair = pltpu.SemaphoreType.DMA((2,))
    block = pltpu.VMEM((size, size), BF16)
    inner, turned = call(
        inner_kernel, [array(planes, size, size), array(size, size, dtype=F32)], [smem()] + [vmem()] * 4, [], 3.2, 12
    )(v_pattern, v_d_near, v_u_near, p_d_near, p_u_near)
    parcel = pltpu.VMEM((planes, live, size), BF16)
    to_next, to_prev = call(
        outward_kernel,
        [array(planes, live, size)] * 2,
        [smem()] + [vmem()] * 4,
        [idx, strip, pltpu.VMEM((2, planes, live, size), BF16), pltpu.SemaphoreType.DMA((2, 4))],
        2,
        10,
        hbm,
    )(present_next, turned, v_u_prev, p_u_near, inner)
    after = shifted(to_prev, -1)
    before = shifted(to_next, 1)

    send_green = call(
        pack_kernel,
        array(routes, LANES),
        [smem(), vmem()],
        [idx, turn, pltpu.VMEM((routes, LANES), BF16), pltpu.SemaphoreType.DMA((tiles,))],
        0.3,
        8,
        hbm,
    )(present, green)
    got_green = routed(send_green.reshape(peers, units, planes, LANES))

    stacked = pltpu.VMEM((flat, size), BF16)
    own = call(
        local_kernel,
        array(planes, live, size),
        [smem()] * 2 + [hbm()] * 2 + [vmem()] + [hbm()] * 2,
        [idx, square, strip, strip, stacked, stacked, whole, whole, block, block, sems, pair],
        5,
        16,
    )(present, v_pattern, v_u_here, v_d_here, v_d_next, p_d, p_u)

    green_freq = call(
        functools.partial(spectrum_kernel, 1.0 / (energies * math.sqrt(energies))),
        array(-(-units // 2), 2 * energies, 2 * LANES, dtype=F32),
        [vmem(), vmem()],
        [],
        0.5,
        8,
    )(forward, got_green)

    send = call(
        join_kernel,
        array(routes, LANES),
        [smem(), vmem()] + [hbm()] * 3,
        [parcel, parcel, block, total, pltpu.SemaphoreType.DMA((2, 2)), pair],
        1,
        12,
    )(v_pattern, own, stay(before), stay(after), v_u_here)
    got = routed(send.reshape(peers, units, planes, LANES))
    result = call(
        convolve_kernel, array(peers, units, planes, LANES), [vmem()] * 4, [], 1, 10
    )(forward, inverse, green_freq, got)
    returned = routed(result).reshape(routes, LANES)

    sigma = call(
        unpack_kernel,
        array(planes, size, size),
        [smem(), vmem()],
        [turn, whole, pltpu.SemaphoreType.DMA((4,))],
        0.3,
        8,
        hbm,
    )(present, returned)
    return sigma.reshape(halves, local, 1, size, size)


def solution(mesh):
    in_specs = (
        P(None, "energy", "space", None, None),
        P(None, "energy", "space", None, None),
        P(None, "energy", "space", None, None),
        P("space", None, None),
        P("space", None, None),
        P("space"),
        P("space", None),
    )
    out_specs = P(None, "energy", "space", None, None)

    return jax.shard_map(per_device, mesh=mesh, in_specs=in_specs, out_specs=out_specs, check_vma=False)
```

```python
import functools
import math

import jax
import jax.numpy as jnp
import numpy as np
from jax import lax
from jax.experimental import pallas as pl
from jax.experimental.pallas import tpu as pltpu
from jax.sharding import PartitionSpec as P


LIVE = 30
RG = 8
LANES = 128

F32 = jnp.float32
BF16 = jnp.bfloat16


def smem():
    return pl.BlockSpec(memory_space=pltpu.SMEM)


def vmem():
    return pl.BlockSpec(memory_space=pltpu.VMEM)


def hbm():
    return pl.BlockSpec(memory_space=pltpu.HBM)


def shifted(value, steps):
    count = lax.axis_size("space")
    pairs = [(source, (source + steps) % count) for source in range(count)]
    return lax.ppermute(value, "space", pairs)


def routed(value):
    return lax.all_to_all(value, "energy", split_axis=0, concat_axis=0, tiled=True)


def dot(left, right):
    return lax.dot_general(left, right, (((1,), (0,)), ((), ())), preferred_element_type=F32)


def dot_nt(left, right):
    return lax.dot_general(left, right, (((1,), (1,)), ((), ())), preferred_element_type=F32)


def tables(energies, peers):
    local = energies // peers
    src, half, step = np.meshgrid(np.arange(peers), np.arange(2), np.arange(local), indexing="ij")
    time = (src * local + step).reshape(-1)
    half = half.reshape(-1)
    freq = np.arange(energies)
    angles = 2.0 * math.pi / energies * ((freq[:, None] * time[None, :]) % energies)
    cosine, sine = np.cos(angles), np.sin(angles)
    real_part = np.where(half == 0, cosine, sine)
    imag_part = np.where(half == 0, -sine, cosine)
    forward = np.concatenate([real_part, imag_part], 0)
    real_out = np.concatenate([-sine, -cosine], 0).T
    imag_out = np.concatenate([cosine, -sine], 0).T
    inverse = np.where((half == 0)[:, None], real_out, imag_out)
    return jnp.asarray(forward, BF16), jnp.asarray(inverse, BF16)


def fetch(sources, targets, sems):
    copies = [pltpu.make_async_copy(a, b, sem) for a, b, sem in zip(sources, targets, sems)]
    for copy in copies:
        copy.start()
    return copies


def arrive(copies):
    for copy in copies:
        copy.wait()


def spread(dest_ref, plane, planes, value):
    rows = value.shape[0]
    for j in range(value.shape[1] // LANES):
        dest_ref[j, pl.ds(plane, rows, stride=planes), :] = value[:, j * LANES : (j + 1) * LANES]


def live_list(present_ref, idx_ref):
    for slot in range(LIVE):
        idx_ref[slot] = 0
    count = jnp.int32(0)
    for group in range(present_ref.shape[0]):
        idx_ref[count] = group
        count = count + jnp.where(present_ref[group] > 0, 1, 0)
    return count


def pick_rows(idx_ref, source_ref, dest_ref):
    for slot in range(LIVE):
        row = pl.multiple_of(idx_ref[slot] * RG, RG)
        dest_ref[slot * RG : (slot + 1) * RG, :] = source_ref[pl.ds(row, RG), :]


def pack_kernel(present_ref, g_ref, out_hbm, idx_ref, turn_ref, ready, sem):
    planes = g_ref.shape[0]
    tiles = g_ref.shape[2] // LANES
    span = LIVE * RG * planes
    live_list(present_ref, idx_ref)
    copies = []
    for tile in range(tiles):
        cols = slice(tile * LANES, (tile + 1) * LANES)
        for slot in range(LIVE):
            turn = turn_ref.at[slot % turn_ref.shape[0]]
            row = pl.multiple_of(idx_ref[slot] * RG, RG)
            for plane in range(planes):
                turn[pl.ds(plane, RG, stride=planes), :] = g_ref[plane, pl.ds(row, RG), cols].astype(F32)
            at = tile * span + slot * RG * planes
            ready[at : at + RG * planes, :] = turn[...].astype(BF16)
        end = (tile + 1) * span
        if tile == tiles - 1:
            ready[end:, :] = jnp.zeros((ready.shape[0] - end, LANES), BF16)
            end = ready.shape[0]
        rows = slice(tile * span, end)
        copies += fetch([ready.at[rows]], [out_hbm.at[rows]], [sem.at[tile]])
    arrive(copies)


def inner_kernel(pattern_ref, vd_ref, vu_ref, pd_ref, pu_ref, out_ref, turned_ref):
    scale = pattern_ref[0].astype(F32)
    turned = (vu_ref[...].astype(F32) * scale).T
    turned_ref[...] = turned
    right = jnp.concatenate([vd_ref[...], turned.astype(BF16)], axis=0)
    for plane in range(pu_ref.shape[0]):
        left = jnp.concatenate([pd_ref[plane], pu_ref[plane]], axis=1)
        out_ref[plane] = dot(left, right).astype(BF16)


def prepare_kernel(present_ref, pattern_ref, vu_ref, out_ref, idx_ref, wide, picked):
    live_list(present_ref, idx_ref)
    wide[...] = vu_ref[...].astype(F32) * pattern_ref[0].astype(F32)
    pick_rows(idx_ref, wide, picked)
    out_ref[...] = picked[...].astype(BF16)


def outward_kernel(half, *refs):
    if half == 0:
        next_ref, turned_ref, left_ref, pu_ref, inner_ref, to_next, to_prev, picked_ref, idx, picked, ready, sem = refs
    else:
        picked_ref, left_ref, pu_ref, inner_ref, to_next, to_prev, ready, sem = refs
    planes = ready.shape[1]
    left_prev = left_ref[...]
    copies = []
    for way, (right_ref, out_hbm) in enumerate(((inner_ref, to_prev), (pu_ref, to_next))):
        left = left_prev
        if way == 1 and half == 0:
            live_list(next_ref, idx)
            pick_rows(idx, turned_ref, picked)
            left = picked[...].astype(BF16)
            picked_ref[...] = left
        elif way == 1:
            left = picked_ref[...]
        for plane in range(planes):
            ready[way, plane] = dot(left, right_ref[half * planes + plane]).astype(BF16)
            if plane % 2 == 1:
                some = slice(plane - 1, plane + 1)
                copies += fetch([ready.at[way, some]], [out_hbm.at[some]], [sem.at[way, plane // 2]])
    arrive(copies)


def local_kernel(
    present_ref,
    pattern_ref,
    vu_hbm,
    vd_hbm,
    vd_next_ref,
    pd_hbm,
    pu_hbm,
    low_ref,
    high_ref,
    idx_ref,
    wide,
    picked_u,
    picked_d,
    same,
    one_up,
    pd_ref,
    pu_ref,
    vd_ref,
    vu_ref,
    sem,
    v_sem,
):
    planes = pu_ref.shape[0]
    rows = LIVE * RG
    small = fetch([vd_hbm, vu_hbm], [vd_ref, vu_ref], [v_sem.at[0], v_sem.at[1]])
    copies = [
        fetch(
            [pd_hbm.at[plane], pu_hbm.at[plane]],
            [pd_ref.at[plane], pu_ref.at[plane]],
            [sem.at[0, plane], sem.at[1, plane]],
        )
        for plane in range(planes)
    ]
    live_list(present_ref, idx_ref)
    arrive(small)
    wide[...] = vu_ref[...].astype(F32) * pattern_ref[0].astype(F32)
    masked = wide[...].astype(BF16)
    pick_rows(idx_ref, wide, picked_u)
    wide[...] = vd_ref[...].astype(F32)
    pick_rows(idx_ref, wide, picked_d)
    left_u = picked_u[...].astype(BF16)
    left_d = picked_d[...].astype(BF16)
    for plane in range(planes):
        arrive(copies[plane])
        at = slice(plane * rows, (plane + 1) * rows)
        same[at] = (dot(left_d, pd_ref[plane]) + dot_nt(left_u, pu_ref[plane])).astype(BF16)
        one_up[at] = dot(left_d, pu_ref[plane]).astype(BF16)
    for plane in range(planes):
        at = slice(plane * rows, (plane + 1) * rows)
        value = dot(same[at], masked) + dot(one_up[at], vd_next_ref[...])
        if plane < planes // 2:
            value = value + picked_u[...]
        out_ref = low_ref if plane < planes // 2 else high_ref
        out_ref[plane % (planes // 2)] = value.astype(BF16)


def join_kernel(pattern_ref, local_ref, before_hbm, after_hbm, vu_hbm, *refs):
    first_ref = refs[0] if len(refs) == 8 else None
    out_ref, before, after, vu_ref = refs[-7:-3] if first_ref is not None else refs[:4]
    sem, v_sem = refs[-2:]
    planes, rows, cols = local_ref.shape
    scale = pattern_ref[0].astype(F32)
    small = fetch([vu_hbm], [vu_ref], [v_sem.at[0]])
    copies = fetch([before_hbm, after_hbm], [before, after], [sem.at[0], sem.at[1]])
    if first_ref is not None:
        total = refs[-3]
        size = total.shape[0] * total.shape[1]
        out_ref[size:, :] = jnp.zeros((out_ref.shape[0] - size, LANES), BF16)
        for plane in range(planes):
            spread(total, plane, 2 * planes, first_ref[plane].astype(F32))
    arrive(small)
    masked = (vu_ref[...].astype(F32) * scale).astype(BF16)
    arrive(copies)
    value = dot(before[...].reshape(planes * rows, cols), masked)
    for plane in range(planes):
        rest = after[plane].astype(F32) * scale + local_ref[plane].astype(F32)
        whole = value[plane * rows : (plane + 1) * rows] + rest
        if first_ref is None:
            out_ref[plane] = whole.astype(BF16)
        else:
            spread(total, planes + plane, 2 * planes, whole)
    if first_ref is not None:
        for tile in range(total.shape[0]):
            at = slice(tile * total.shape[1], (tile + 1) * total.shape[1])
            out_ref[at, :] = total[tile].astype(BF16)


def unit_pairs(got_ref):
    peers, units, planes, lanes = got_ref.shape
    for first in range(0, units, 2):
        some = range(first, min(first + 2, units))
        yield first, [got_ref[:, unit].reshape(peers * planes, lanes) for unit in some]


def spectrum_kernel(scale, forward_ref, got_ref, out_ref):
    for first, values in unit_pairs(got_ref):
        width = LANES * len(values)
        out_ref[first // 2, :, :width] = dot(forward_ref[...], jnp.concatenate(values, 1)) * scale


def convolve_kernel(forward_ref, inverse_ref, green_ref, got_ref, out_ref):
    peers, _, planes, lanes = got_ref.shape
    half = forward_ref.shape[0] // 2
    for first, values in unit_pairs(got_ref):
        width = LANES * len(values)
        freq = dot(forward_ref[...], jnp.concatenate(values, 1))
        green_re, green_im = green_ref[first // 2, :half, :width], green_ref[first // 2, half:, :width]
        screen_re, screen_im = freq[:half], freq[half:]
        mixed = jnp.concatenate(
            [green_re * screen_re - green_im * screen_im, green_re * screen_im + green_im * screen_re], 0
        )
        result = dot(inverse_ref[...], mixed.astype(BF16)).astype(BF16)
        for at in range(len(values)):
            out_ref[:, first + at] = result[:, at * lanes : (at + 1) * lanes].reshape(peers, planes, lanes)


def unpack_kernel(present_ref, got_ref, out_hbm, turn_ref, ready, sem):
    groups = present_ref.shape[0]
    planes, _, cols = ready.shape
    tiles = cols // LANES
    span = LIVE * RG * planes
    batch = groups // sem.shape[0]
    copies = []
    slot = jnp.int32(0)
    for group in range(groups):
        rows = slice(group * RG, (group + 1) * RG)

        @pl.when(present_ref[group] > 0)
        def _(slot=slot, rows=rows):
            for tile in range(tiles):
                turn = turn_ref.at[tile]
                at = pl.multiple_of(tile * span + slot * RG * planes, RG * planes)
                turn[...] = got_ref[pl.ds(at, RG * planes), :].astype(F32)
                for plane in range(planes):
                    value = turn[pl.ds(plane, RG, stride=planes), :]
                    ready[plane, rows, tile * LANES : (tile + 1) * LANES] = value.astype(BF16)

        @pl.when(present_ref[group] <= 0)
        def _(rows=rows):
            ready[:, rows, :] = jnp.zeros((planes, RG, cols), BF16)

        slot = slot + jnp.where(present_ref[group] > 0, 1, 0)
        if group % batch == batch - 1:
            some = slice((group + 1 - batch) * RG, (group + 1) * RG)
            copies += fetch([ready.at[:, some]], [out_hbm.at[:, some]], [sem.at[group // batch]])
    arrive(copies)


def per_device(g_upper, p_diag, p_upper, v_diag, v_upper, v_pattern, element_present):
    peers = lax.axis_size("energy")
    halves, local, _, size, _ = g_upper.shape
    planes = halves * local
    energies = local * peers
    live = LIVE * RG
    flat = live * planes

    def stay(value):
        return pltpu.with_memory_space_constraint(value, pltpu.HBM)

    p_d, p_u = (stay(x.reshape(planes, size, size)) for x in (p_diag, p_upper))
    v_d, v_u = (x.reshape(size, size) for x in (v_diag, v_upper))
    v_d_here, v_u_here = stay(v_d), stay(v_u)

    def near(value):
        return pltpu.with_memory_space_constraint(value, pltpu.VMEM)

    p_d_near, p_u_near, green = (
        near(x.reshape(planes, size, size)) for x in (p_diag, p_upper, g_upper)
    )
    v_d_near, v_u_near = near(v_d), near(v_u)
    present = element_present.reshape(-1)
    groups = present.shape[0]
    tiles = size // LANES
    units = -(-live * tiles // peers)
    routes = peers * units * planes

    idx = pltpu.SMEM((groups,), jnp.int32)
    square = pltpu.VMEM((size, size), F32)
    strip = pltpu.VMEM((live, size), F32)
    total = pltpu.VMEM((size // LANES, flat, LANES), F32)
    turn = pltpu.VMEM((6, RG * planes, LANES), F32)
    big = planes * size * size * 2

    def call(kernel, outs, ins, scratch, units, mib, places=None):
        if places is None:
            places = [vmem() for _ in outs] if isinstance(outs, list) else vmem()
        return pl.pallas_call(
            kernel,
            out_shape=outs,
            in_specs=ins,
            out_specs=places,
            scratch_shapes=scratch,
            compiler_params=pltpu.CompilerParams(vmem_limit_bytes=mib * 2**20),
            cost_estimate=pl.CostEstimate(
                flops=int(units * 2 * planes * live * size * size), bytes_accessed=int(big), transcendentals=0
            ),
        )

    def array(*shape, dtype=BF16):
        return jax.ShapeDtypeStruct(shape, dtype)

    chosen = call(
        prepare_kernel, array(live, size), [smem()] * 2 + [vmem()], [idx, square, strip], 8, 6
    )(present, v_pattern, v_u)
    v_u_prev = shifted(chosen, 1)
    present_next = shifted(present, -1)
    v_d_next = shifted(v_d, -1)
    forward, inverse = tables(energies, peers)

    whole = pltpu.VMEM((planes, size, size), BF16)
    sems = pltpu.SemaphoreType.DMA((2, planes))
    pair = pltpu.SemaphoreType.DMA((2,))
    block = pltpu.VMEM((size, size), BF16)
    inner, turned = call(
        inner_kernel,
        [array(planes, size, size), array(size, size, dtype=F32)],
        [smem()] + [vmem()] * 4,
        [],
        3.2,
        12,
    )(v_pattern, v_d_near, v_u_near, p_d_near, p_u_near)
    half = planes // 2
    parcel = pltpu.VMEM((half, live, size), BF16)
    moving = [pltpu.VMEM((2, half, live, size), BF16), pltpu.SemaphoreType.DMA((2, half // 2))]

    def outward(part, ins, outs, specs, scratch):
        kernel = functools.partial(outward_kernel, part)
        places = [hbm(), hbm()] + [vmem()] * (len(outs) - 2)
        return call(kernel, outs, specs, scratch + moving, 1, 8, places)(*ins)

    leaving = [array(half, live, size)] * 2
    to_next, to_prev, picked = outward(
        0,
        [present_next, turned, v_u_prev, p_u_near, inner],
        leaving + [array(live, size)],
        [smem()] + [vmem()] * 4,
        [idx, strip],
    )
    after, before = [shifted(to_prev, -1)], [shifted(to_next, 1)]
    to_next, to_prev = outward(1, [picked, v_u_prev, p_u_near, inner], leaving, [vmem()] * 4, [])
    after.append(shifted(to_prev, -1))
    before.append(shifted(to_next, 1))

    send_green = call(
        pack_kernel,
        array(routes, LANES),
        [smem(), vmem()],
        [idx, turn, pltpu.VMEM((routes, LANES), BF16), pltpu.SemaphoreType.DMA((tiles,))],
        0.3,
        8,
        hbm(),
    )(present, green)
    got_green = routed(send_green.reshape(peers, units, planes, LANES))

    stacked = pltpu.VMEM((flat, size), BF16)
    own = call(
        local_kernel,
        [array(half, live, size)] * 2,
        [smem()] * 2 + [hbm()] * 2 + [vmem()] + [hbm()] * 2,
        [idx, square, strip, strip, stacked, stacked, whole, whole, block, block, sems, pair],
        5,
        16,
    )(present, v_pattern, v_u_here, v_d_here, v_d_next, p_d, p_u)

    green_freq = call(
        functools.partial(spectrum_kernel, 1.0 / (energies * math.sqrt(energies))),
        array(-(-units // 2), 2 * energies, 2 * LANES, dtype=F32),
        [vmem(), vmem()],
        [],
        0.5,
        8,
    )(forward, got_green)

    scratch = [parcel, parcel, block]
    partial = call(
        join_kernel,
        array(half, live, size),
        [smem(), vmem()] + [hbm()] * 3,
        scratch + [pair, pair],
        0.5,
        6,
    )(v_pattern, own[0], stay(before[0]), stay(after[0]), v_u_here)
    send = call(
        join_kernel,
        array(routes, LANES),
        [smem(), vmem()] + [hbm()] * 3 + [vmem()],
        scratch + [total, pair, pair],
        0.5,
        10,
    )(v_pattern, own[1], stay(before[1]), stay(after[1]), v_u_here, partial)
    got = routed(send.reshape(peers, units, planes, LANES))
    result = call(
        convolve_kernel, array(peers, units, planes, LANES), [vmem()] * 4, [], 1, 10
    )(forward, inverse, green_freq, got)
    returned = routed(result).reshape(routes, LANES)

    sigma = call(
        unpack_kernel,
        array(planes, size, size),
        [smem(), vmem()],
        [turn, whole, pltpu.SemaphoreType.DMA((4,))],
        0.3,
        8,
        hbm(),
    )(present, returned)
    return sigma.reshape(halves, local, 1, size, size)


def solution(mesh):
    in_specs = (
        P(None, "energy", "space", None, None),
        P(None, "energy", "space", None, None),
        P(None, "energy", "space", None, None),
        P("space", None, None),
        P("space", None, None),
        P("space"),
        P("space", None),
    )
    out_specs = P(None, "energy", "space", None, None)

    return jax.shard_map(per_device, mesh=mesh, in_specs=in_specs, out_specs=out_specs, check_vma=False)
```

```python
import functools
import math

import jax
import jax.numpy as jnp
import numpy as np
from jax import lax
from jax.experimental import pallas as pl
from jax.experimental.pallas import tpu as pltpu
from jax.sharding import PartitionSpec as P


LIVE = 30
RG = 8
LANES = 128

F32 = jnp.float32
BF16 = jnp.bfloat16


def smem():
    return pl.BlockSpec(memory_space=pltpu.SMEM)


def vmem():
    return pl.BlockSpec(memory_space=pltpu.VMEM)


def hbm():
    return pl.BlockSpec(memory_space=pltpu.HBM)


def shifted(value, steps):
    count = lax.axis_size("space")
    pairs = [(source, (source + steps) % count) for source in range(count)]
    return lax.ppermute(value, "space", pairs)


def routed(value):
    return lax.all_to_all(value, "energy", split_axis=0, concat_axis=0, tiled=True)


def dot(left, right):
    return lax.dot_general(left, right, (((1,), (0,)), ((), ())), preferred_element_type=F32)


def dot_nt(left, right):
    return lax.dot_general(left, right, (((1,), (1,)), ((), ())), preferred_element_type=F32)


def tables(energies, peers):
    local = energies // peers
    src, half, step = np.meshgrid(np.arange(peers), np.arange(2), np.arange(local), indexing="ij")
    time = (src * local + step).reshape(-1)
    half = half.reshape(-1)
    freq = np.arange(energies)
    angles = 2.0 * math.pi / energies * ((freq[:, None] * time[None, :]) % energies)
    cosine, sine = np.cos(angles), np.sin(angles)
    real_part = np.where(half == 0, cosine, sine)
    imag_part = np.where(half == 0, -sine, cosine)
    forward = np.concatenate([real_part, imag_part], 0)
    real_out = np.concatenate([-sine, -cosine], 0).T
    imag_out = np.concatenate([cosine, -sine], 0).T
    inverse = np.where((half == 0)[:, None], real_out, imag_out)
    return jnp.asarray(forward, BF16), jnp.asarray(inverse, BF16)


def fetch(sources, targets, sems):
    copies = [pltpu.make_async_copy(a, b, sem) for a, b, sem in zip(sources, targets, sems)]
    for copy in copies:
        copy.start()
    return copies


def arrive(copies):
    for copy in copies:
        copy.wait()


def spread(dest_ref, plane, planes, value):
    rows = value.shape[0]
    for j in range(value.shape[1] // LANES):
        dest_ref[j, pl.ds(plane, rows, stride=planes), :] = value[:, j * LANES : (j + 1) * LANES]


def live_list(present_ref, idx_ref):
    for slot in range(LIVE):
        idx_ref[slot] = 0
    count = jnp.int32(0)
    for group in range(present_ref.shape[0]):
        idx_ref[count] = group
        count = count + jnp.where(present_ref[group] > 0, 1, 0)
    return count


def pick_rows(idx_ref, source_ref, dest_ref):
    for slot in range(LIVE):
        row = pl.multiple_of(idx_ref[slot] * RG, RG)
        dest_ref[slot * RG : (slot + 1) * RG, :] = source_ref[pl.ds(row, RG), :]


def pack_kernel(present_ref, g_ref, out_hbm, idx_ref, turn_ref, ready, sem):
    planes = g_ref.shape[0]
    tiles, span, _ = turn_ref.shape
    live_list(present_ref, idx_ref)
    copies = []
    for tile in range(tiles):
        cols = slice(tile * LANES, (tile + 1) * LANES)
        for slot in range(LIVE):
            row = pl.multiple_of(idx_ref[slot] * RG, RG)
            for plane in range(planes):
                at = slot * RG * planes + plane
                value = g_ref[plane, pl.ds(row, RG), cols].astype(F32)
                turn_ref[tile, pl.ds(at, RG, stride=planes), :] = value
        ready[tile * span : (tile + 1) * span, :] = turn_ref[tile].astype(BF16)
        end = (tile + 1) * span
        if tile == tiles - 1:
            ready[end:, :] = jnp.zeros((ready.shape[0] - end, LANES), BF16)
            end = ready.shape[0]
        rows = slice(tile * span, end)
        copies += fetch([ready.at[rows]], [out_hbm.at[rows]], [sem.at[tile]])
    arrive(copies)


def inner_kernel(pattern_ref, vd_ref, vu_ref, pd_ref, pu_ref, out_ref, turned_ref):
    scale = pattern_ref[0].astype(F32)
    turned = (vu_ref[...].astype(F32) * scale).T
    turned_ref[...] = turned
    right = jnp.concatenate([vd_ref[...], turned.astype(BF16)], axis=0)
    for plane in range(pu_ref.shape[0]):
        left = jnp.concatenate([pd_ref[plane], pu_ref[plane]], axis=1)
        out_ref[plane] = dot(left, right).astype(BF16)


def prepare_kernel(present_ref, pattern_ref, vu_ref, out_ref, idx_ref, wide, picked):
    live_list(present_ref, idx_ref)
    wide[...] = vu_ref[...].astype(F32) * pattern_ref[0].astype(F32)
    pick_rows(idx_ref, wide, picked)
    out_ref[...] = picked[...].astype(BF16)


def outward_kernel(half, *refs):
    if half == 0:
        next_ref, turned_ref, left_ref, pu_ref, inner_ref, to_next, to_prev, picked_ref, idx, picked, ready, sem = refs
    else:
        picked_ref, left_ref, pu_ref, inner_ref, to_next, to_prev, ready, sem = refs
    planes = ready.shape[1]
    left_prev = left_ref[...]
    copies = []
    for way, (right_ref, out_hbm) in enumerate(((inner_ref, to_prev), (pu_ref, to_next))):
        left = left_prev
        if way == 1 and half == 0:
            live_list(next_ref, idx)
            pick_rows(idx, turned_ref, picked)
            left = picked[...].astype(BF16)
            picked_ref[...] = left
        elif way == 1:
            left = picked_ref[...]
        for plane in range(planes):
            ready[way, plane] = dot(left, right_ref[half * planes + plane]).astype(BF16)
            if plane % 2 == 1:
                some = slice(plane - 1, plane + 1)
                copies += fetch([ready.at[way, some]], [out_hbm.at[some]], [sem.at[way, plane // 2]])
    arrive(copies)


def local_kernel(
    present_ref,
    pattern_ref,
    vu_hbm,
    vd_hbm,
    vd_next_ref,
    pd_hbm,
    pu_hbm,
    low_ref,
    high_ref,
    idx_ref,
    wide,
    picked_u,
    picked_d,
    same,
    one_up,
    pd_ref,
    pu_ref,
    vd_ref,
    vu_ref,
    sem,
    v_sem,
):
    planes = pu_ref.shape[0]
    rows = LIVE * RG
    small = fetch([vd_hbm, vu_hbm], [vd_ref, vu_ref], [v_sem.at[0], v_sem.at[1]])
    copies = [
        fetch(
            [pd_hbm.at[plane], pu_hbm.at[plane]],
            [pd_ref.at[plane], pu_ref.at[plane]],
            [sem.at[0, plane], sem.at[1, plane]],
        )
        for plane in range(planes)
    ]
    live_list(present_ref, idx_ref)
    arrive(small)
    wide[...] = vu_ref[...].astype(F32) * pattern_ref[0].astype(F32)
    masked = wide[...].astype(BF16)
    pick_rows(idx_ref, wide, picked_u)
    wide[...] = vd_ref[...].astype(F32)
    pick_rows(idx_ref, wide, picked_d)
    left_u = picked_u[...].astype(BF16)
    left_d = picked_d[...].astype(BF16)
    for plane in range(planes):
        arrive(copies[plane])
        at = slice(plane * rows, (plane + 1) * rows)
        same[at] = (dot(left_d, pd_ref[plane]) + dot_nt(left_u, pu_ref[plane])).astype(BF16)
        one_up[at] = dot(left_d, pu_ref[plane]).astype(BF16)
    for plane in range(planes):
        at = slice(plane * rows, (plane + 1) * rows)
        value = dot(same[at], masked) + dot(one_up[at], vd_next_ref[...])
        if plane < planes // 2:
            value = value + picked_u[...]
        out_ref = low_ref if plane < planes // 2 else high_ref
        out_ref[plane % (planes // 2)] = value.astype(BF16)


def join_kernel(pattern_ref, local_ref, before_hbm, after_hbm, vu_hbm, *refs):
    first_ref = refs[0] if len(refs) == 8 else None
    out_ref, before, after, vu_ref = refs[-7:-3] if first_ref is not None else refs[:4]
    sem, v_sem = refs[-2:]
    planes, rows, cols = local_ref.shape
    scale = pattern_ref[0].astype(F32)
    small = fetch([vu_hbm], [vu_ref], [v_sem.at[0]])
    copies = fetch([before_hbm, after_hbm], [before, after], [sem.at[0], sem.at[1]])
    if first_ref is not None:
        total = refs[-3]
        size = total.shape[0] * total.shape[1]
        out_ref[size:, :] = jnp.zeros((out_ref.shape[0] - size, LANES), BF16)
        for plane in range(planes):
            spread(total, plane, 2 * planes, first_ref[plane].astype(F32))
    arrive(small)
    masked = (vu_ref[...].astype(F32) * scale).astype(BF16)
    arrive(copies)
    value = dot(before[...].reshape(planes * rows, cols), masked)
    for plane in range(planes):
        rest = after[plane].astype(F32) * scale + local_ref[plane].astype(F32)
        whole = value[plane * rows : (plane + 1) * rows] + rest
        if first_ref is None:
            out_ref[plane] = whole.astype(BF16)
        else:
            spread(total, planes + plane, 2 * planes, whole)
    if first_ref is not None:
        for tile in range(total.shape[0]):
            at = slice(tile * total.shape[1], (tile + 1) * total.shape[1])
            out_ref[at, :] = total[tile].astype(BF16)


def unit_pairs(got_ref):
    peers, units, planes, lanes = got_ref.shape
    for first in range(0, units, 2):
        some = range(first, min(first + 2, units))
        yield first, [got_ref[:, unit].reshape(peers * planes, lanes) for unit in some]


def spectrum_kernel(scale, forward_ref, got_ref, out_ref):
    for first, values in unit_pairs(got_ref):
        width = LANES * len(values)
        out_ref[first // 2, :, :width] = dot(forward_ref[...], jnp.concatenate(values, 1)) * scale


def convolve_kernel(forward_ref, inverse_ref, green_ref, got_ref, out_ref):
    peers, _, planes, lanes = got_ref.shape
    half = forward_ref.shape[0] // 2
    for first, values in unit_pairs(got_ref):
        width = LANES * len(values)
        freq = dot(forward_ref[...], jnp.concatenate(values, 1))
        green_re, green_im = green_ref[first // 2, :half, :width], green_ref[first // 2, half:, :width]
        screen_re, screen_im = freq[:half], freq[half:]
        mixed = jnp.concatenate(
            [green_re * screen_re - green_im * screen_im, green_re * screen_im + green_im * screen_re], 0
        )
        result = dot(inverse_ref[...], mixed.astype(BF16)).astype(BF16)
        for at in range(len(values)):
            out_ref[:, first + at] = result[:, at * lanes : (at + 1) * lanes].reshape(peers, planes, lanes)


def unpack_kernel(present_ref, got_ref, out_hbm, turn_ref, ready, sem):
    groups = present_ref.shape[0]
    planes, _, cols = ready.shape
    tiles = cols // LANES
    span = LIVE * RG * planes
    batch = groups // sem.shape[0]
    for tile in range(tiles):
        turn_ref[tile, :span] = got_ref[tile * span : (tile + 1) * span, :].astype(F32)
    copies = []
    slot = jnp.int32(0)
    for group in range(groups):
        rows = slice(group * RG, (group + 1) * RG)
        live = present_ref[group] > 0
        at = pl.multiple_of(slot * RG * planes, RG * planes)
        for tile in range(tiles):
            for plane in range(planes):
                value = turn_ref[tile, pl.ds(at + plane, RG, stride=planes), :]
                value = jnp.where(live, value, 0.0).astype(BF16)
                ready[plane, rows, tile * LANES : (tile + 1) * LANES] = value
        slot = slot + jnp.where(live, 1, 0)
        if group % batch == batch - 1:
            some = slice((group + 1 - batch) * RG, (group + 1) * RG)
            copies += fetch([ready.at[:, some]], [out_hbm.at[:, some]], [sem.at[group // batch]])
    arrive(copies)


def per_device(g_upper, p_diag, p_upper, v_diag, v_upper, v_pattern, element_present):
    peers = lax.axis_size("energy")
    halves, local, _, size, _ = g_upper.shape
    planes = halves * local
    energies = local * peers
    live = LIVE * RG
    flat = live * planes

    def stay(value):
        return pltpu.with_memory_space_constraint(value, pltpu.HBM)

    p_d, p_u = (stay(x.reshape(planes, size, size)) for x in (p_diag, p_upper))
    v_d, v_u = (x.reshape(size, size) for x in (v_diag, v_upper))
    v_d_here, v_u_here = stay(v_d), stay(v_u)

    def near(value):
        return pltpu.with_memory_space_constraint(value, pltpu.VMEM)

    p_d_near, p_u_near, green = (
        near(x.reshape(planes, size, size)) for x in (p_diag, p_upper, g_upper)
    )
    v_d_near, v_u_near = near(v_d), near(v_u)
    present = element_present.reshape(-1)
    groups = present.shape[0]
    tiles = size // LANES
    units = -(-live * tiles // peers)
    routes = peers * units * planes

    idx = pltpu.SMEM((groups,), jnp.int32)
    square = pltpu.VMEM((size, size), F32)
    strip = pltpu.VMEM((live, size), F32)
    total = pltpu.VMEM((size // LANES, flat, LANES), F32)
    big = planes * size * size * 2

    def call(kernel, outs, ins, scratch, units, mib, places=None):
        if places is None:
            places = [vmem() for _ in outs] if isinstance(outs, list) else vmem()
        return pl.pallas_call(
            kernel,
            out_shape=outs,
            in_specs=ins,
            out_specs=places,
            scratch_shapes=scratch,
            compiler_params=pltpu.CompilerParams(vmem_limit_bytes=mib * 2**20),
            cost_estimate=pl.CostEstimate(
                flops=int(units * 2 * planes * live * size * size), bytes_accessed=int(big), transcendentals=0
            ),
        )

    def array(*shape, dtype=BF16):
        return jax.ShapeDtypeStruct(shape, dtype)

    chosen = call(
        prepare_kernel, array(live, size), [smem()] * 2 + [vmem()], [idx, square, strip], 8, 6
    )(present, v_pattern, v_u)
    v_u_prev = shifted(chosen, 1)
    present_next = shifted(present, -1)
    v_d_next = shifted(v_d, -1)
    forward, inverse = tables(energies, peers)

    whole = pltpu.VMEM((planes, size, size), BF16)
    sems = pltpu.SemaphoreType.DMA((2, planes))
    pair = pltpu.SemaphoreType.DMA((2,))
    block = pltpu.VMEM((size, size), BF16)
    inner, turned = call(
        inner_kernel,
        [array(planes, size, size), array(size, size, dtype=F32)],
        [smem()] + [vmem()] * 4,
        [],
        3.2,
        12,
    )(v_pattern, v_d_near, v_u_near, p_d_near, p_u_near)
    half = planes // 2
    parcel = pltpu.VMEM((half, live, size), BF16)
    moving = [pltpu.VMEM((2, half, live, size), BF16), pltpu.SemaphoreType.DMA((2, half // 2))]

    def outward(part, ins, outs, specs, scratch):
        kernel = functools.partial(outward_kernel, part)
        places = [hbm(), hbm()] + [vmem()] * (len(outs) - 2)
        return call(kernel, outs, specs, scratch + moving, 1, 8, places)(*ins)

    leaving = [array(half, live, size)] * 2
    to_next, to_prev, picked = outward(
        0,
        [present_next, turned, v_u_prev, p_u_near, inner],
        leaving + [array(live, size)],
        [smem()] + [vmem()] * 4,
        [idx, strip],
    )
    after, before = [shifted(to_prev, -1)], [shifted(to_next, 1)]
    to_next, to_prev = outward(1, [picked, v_u_prev, p_u_near, inner], leaving, [vmem()] * 4, [])
    after.append(shifted(to_prev, -1))
    before.append(shifted(to_next, 1))

    send_green = call(
        pack_kernel,
        array(routes, LANES),
        [smem(), vmem()],
        [idx, total, pltpu.VMEM((routes, LANES), BF16), pltpu.SemaphoreType.DMA((tiles,))],
        0.3,
        8,
        hbm(),
    )(present, green)
    got_green = routed(send_green.reshape(peers, units, planes, LANES))

    stacked = pltpu.VMEM((flat, size), BF16)
    own = call(
        local_kernel,
        [array(half, live, size)] * 2,
        [smem()] * 2 + [hbm()] * 2 + [vmem()] + [hbm()] * 2,
        [idx, square, strip, strip, stacked, stacked, whole, whole, block, block, sems, pair],
        5,
        16,
    )(present, v_pattern, v_u_here, v_d_here, v_d_next, p_d, p_u)

    green_freq = call(
        functools.partial(spectrum_kernel, 1.0 / (energies * math.sqrt(energies))),
        array(-(-units // 2), 2 * energies, 2 * LANES, dtype=F32),
        [vmem(), vmem()],
        [],
        0.5,
        8,
    )(forward, got_green)

    scratch = [parcel, parcel, block]
    partial = call(
        join_kernel,
        array(half, live, size),
        [smem(), vmem()] + [hbm()] * 3,
        scratch + [pair, pair],
        0.5,
        6,
    )(v_pattern, own[0], stay(before[0]), stay(after[0]), v_u_here)
    send = call(
        join_kernel,
        array(routes, LANES),
        [smem(), vmem()] + [hbm()] * 3 + [vmem()],
        scratch + [total, pair, pair],
        0.5,
        10,
    )(v_pattern, own[1], stay(before[1]), stay(after[1]), v_u_here, partial)
    got = routed(send.reshape(peers, units, planes, LANES))
    result = call(
        convolve_kernel, array(peers, units, planes, LANES), [vmem()] * 4, [], 1, 10
    )(forward, inverse, green_freq, got)
    returned = routed(result).reshape(routes, LANES)

    sigma = call(
        unpack_kernel,
        array(planes, size, size),
        [smem(), vmem()],
        [pltpu.VMEM((tiles, flat + RG * planes, LANES), F32), whole, pltpu.SemaphoreType.DMA((4,))],
        0.3,
        8,
        hbm(),
    )(present, returned)
    return sigma.reshape(halves, local, 1, size, size)


def solution(mesh):
    in_specs = (
        P(None, "energy", "space", None, None),
        P(None, "energy", "space", None, None),
        P(None, "energy", "space", None, None),
        P("space", None, None),
        P("space", None, None),
        P("space"),
        P("space", None),
    )
    out_specs = P(None, "energy", "space", None, None)

    return jax.shard_map(per_device, mesh=mesh, in_specs=in_specs, out_specs=out_specs, check_vma=False)
```

```python
import functools
import math

import jax
import jax.numpy as jnp
import numpy as np
from jax import lax
from jax.experimental import pallas as pl
from jax.experimental.pallas import tpu as pltpu
from jax.sharding import PartitionSpec as P


LIVE = 30
RG = 8
LANES = 128

F32 = jnp.float32
BF16 = jnp.bfloat16


def smem():
    return pl.BlockSpec(memory_space=pltpu.SMEM)


def vmem():
    return pl.BlockSpec(memory_space=pltpu.VMEM)


def hbm():
    return pl.BlockSpec(memory_space=pltpu.HBM)


def shifted(value, steps):
    count = lax.axis_size("space")
    pairs = [(source, (source + steps) % count) for source in range(count)]
    return lax.ppermute(value, "space", pairs)


def routed(value):
    return lax.all_to_all(value, "energy", split_axis=0, concat_axis=0, tiled=True)


def dot(left, right):
    return lax.dot_general(left, right, (((1,), (0,)), ((), ())), preferred_element_type=F32)


def dot_nt(left, right):
    return lax.dot_general(left, right, (((1,), (1,)), ((), ())), preferred_element_type=F32)


def tables(energies, peers):
    local = energies // peers
    src, half, step = np.meshgrid(np.arange(peers), np.arange(2), np.arange(local), indexing="ij")
    time = (src * local + step).reshape(-1)
    half = half.reshape(-1)
    freq = np.arange(energies)
    angles = 2.0 * math.pi / energies * ((freq[:, None] * time[None, :]) % energies)
    cosine, sine = np.cos(angles), np.sin(angles)
    real_part = np.where(half == 0, cosine, sine)
    imag_part = np.where(half == 0, -sine, cosine)
    forward = np.concatenate([real_part, imag_part], 0)
    real_out = np.concatenate([-sine, -cosine], 0).T
    imag_out = np.concatenate([cosine, -sine], 0).T
    inverse = np.where((half == 0)[:, None], real_out, imag_out)
    return jnp.asarray(forward, BF16), jnp.asarray(inverse, BF16)


def fetch(sources, targets, sems):
    copies = [pltpu.make_async_copy(a, b, sem) for a, b, sem in zip(sources, targets, sems)]
    for copy in copies:
        copy.start()
    return copies


def arrive(copies):
    for copy in copies:
        copy.wait()


def spread(dest_ref, plane, planes, value):
    rows = value.shape[0]
    for j in range(value.shape[1] // LANES):
        dest_ref[j, pl.ds(plane, rows, stride=planes), :] = value[:, j * LANES : (j + 1) * LANES]


def live_list(present_ref, idx_ref):
    for slot in range(LIVE):
        idx_ref[slot] = 0
    count = jnp.int32(0)
    for group in range(present_ref.shape[0]):
        idx_ref[count] = group
        count = count + jnp.where(present_ref[group] > 0, 1, 0)
    return count


def pick_rows(idx_ref, source_ref, dest_ref):
    for slot in range(LIVE):
        row = pl.multiple_of(idx_ref[slot] * RG, RG)
        dest_ref[slot * RG : (slot + 1) * RG, :] = source_ref[pl.ds(row, RG), :]


def pack_kernel(present_ref, g_ref, out_hbm, idx_ref, turn_ref, ready, sem):
    planes = g_ref.shape[0]
    tiles, span, _ = turn_ref.shape
    live_list(present_ref, idx_ref)
    copies = []
    for tile in range(tiles):
        cols = slice(tile * LANES, (tile + 1) * LANES)
        for slot in range(LIVE):
            row = pl.multiple_of(idx_ref[slot] * RG, RG)
            for plane in range(planes):
                at = slot * RG * planes + plane
                value = g_ref[plane, pl.ds(row, RG), cols].astype(F32)
                turn_ref[tile, pl.ds(at, RG, stride=planes), :] = value
        ready[tile * span : (tile + 1) * span, :] = turn_ref[tile].astype(BF16)
        end = (tile + 1) * span
        if tile == tiles - 1:
            ready[end:, :] = jnp.zeros((ready.shape[0] - end, LANES), BF16)
            end = ready.shape[0]
        rows = slice(tile * span, end)
        copies += fetch([ready.at[rows]], [out_hbm.at[rows]], [sem.at[tile]])
    arrive(copies)


def inner_kernel(pattern_ref, vd_ref, vu_ref, pd_ref, pu_ref, out_ref, turned_ref):
    scale = pattern_ref[0].astype(F32)
    turned = (vu_ref[...].astype(F32) * scale).T
    turned_ref[...] = turned
    right = jnp.concatenate([vd_ref[...], turned.astype(BF16)], axis=0)
    for plane in range(pu_ref.shape[0]):
        left = jnp.concatenate([pd_ref[plane], pu_ref[plane]], axis=1)
        out_ref[plane] = dot(left, right).astype(BF16)


def prepare_kernel(present_ref, pattern_ref, vu_hbm, out_ref, idx_ref, held, sem):
    live_list(present_ref, idx_ref)
    copies = []
    for slot in range(LIVE):
        row = pl.multiple_of(idx_ref[slot] * RG, RG)
        target = held.at[pl.ds(slot * RG, RG), :]
        copies += fetch([vu_hbm.at[pl.ds(row, RG), :]], [target], [sem.at[slot]])
    arrive(copies)
    out_ref[...] = (held[...].astype(F32) * pattern_ref[0].astype(F32)).astype(BF16)


def outward_kernel(half, *refs):
    if half == 0:
        next_ref, turned_ref, left_ref, pu_ref, inner_ref, to_next, to_prev, picked_ref, idx, picked, ready, sem = refs
    else:
        picked_ref, left_ref, pu_ref, inner_ref, to_next, to_prev, ready, sem = refs
    planes = ready.shape[1]
    left_prev = left_ref[...]
    copies = []
    for way, (right_ref, out_hbm) in enumerate(((inner_ref, to_prev), (pu_ref, to_next))):
        left = left_prev
        if way == 1 and half == 0:
            live_list(next_ref, idx)
            pick_rows(idx, turned_ref, picked)
            left = picked[...].astype(BF16)
            picked_ref[...] = left
        elif way == 1:
            left = picked_ref[...]
        for plane in range(planes):
            ready[way, plane] = dot(left, right_ref[half * planes + plane]).astype(BF16)
            if plane % 2 == 1:
                some = slice(plane - 1, plane + 1)
                copies += fetch([ready.at[way, some]], [out_hbm.at[some]], [sem.at[way, plane // 2]])
    arrive(copies)


def local_kernel(
    present_ref,
    pattern_ref,
    vu_hbm,
    vd_hbm,
    vd_next_ref,
    pd_hbm,
    pu_hbm,
    low_ref,
    high_ref,
    idx_ref,
    wide,
    picked_u,
    picked_d,
    same,
    one_up,
    pd_ref,
    pu_ref,
    vd_ref,
    vu_ref,
    sem,
    v_sem,
):
    planes = pu_ref.shape[0]
    rows = LIVE * RG
    small = fetch([vd_hbm, vu_hbm], [vd_ref, vu_ref], [v_sem.at[0], v_sem.at[1]])
    copies = [
        fetch(
            [pd_hbm.at[plane], pu_hbm.at[plane]],
            [pd_ref.at[plane], pu_ref.at[plane]],
            [sem.at[0, plane], sem.at[1, plane]],
        )
        for plane in range(planes)
    ]
    live_list(present_ref, idx_ref)
    arrive(small)
    wide[...] = vu_ref[...].astype(F32) * pattern_ref[0].astype(F32)
    masked = wide[...].astype(BF16)
    pick_rows(idx_ref, wide, picked_u)
    wide[...] = vd_ref[...].astype(F32)
    pick_rows(idx_ref, wide, picked_d)
    left_u = picked_u[...].astype(BF16)
    left_d = picked_d[...].astype(BF16)
    for plane in range(planes):
        arrive(copies[plane])
        at = slice(plane * rows, (plane + 1) * rows)
        same[at] = (dot(left_d, pd_ref[plane]) + dot_nt(left_u, pu_ref[plane])).astype(BF16)
        one_up[at] = dot(left_d, pu_ref[plane]).astype(BF16)
    for plane in range(planes):
        at = slice(plane * rows, (plane + 1) * rows)
        value = dot(same[at], masked) + dot(one_up[at], vd_next_ref[...])
        if plane < planes // 2:
            value = value + picked_u[...]
        out_ref = low_ref if plane < planes // 2 else high_ref
        out_ref[plane % (planes // 2)] = value.astype(BF16)


def join_low_kernel(
    pattern_ref, local_ref, before_hbm, after_hbm, vu_hbm, out_ref, masked_ref, before, after, vu_ref, sem
):
    planes, rows, cols = local_ref.shape
    scale = pattern_ref[0].astype(F32)
    copies = fetch([vu_hbm, before_hbm, after_hbm], [vu_ref, before, after], [sem.at[0], sem.at[1], sem.at[2]])
    arrive(copies)
    masked_ref[...] = (vu_ref[...].astype(F32) * scale).astype(BF16)
    value = dot(before[...].reshape(planes * rows, cols), masked_ref[...])
    for plane in range(planes):
        rest = after[plane].astype(F32) * scale + local_ref[plane].astype(F32)
        out_ref[plane] = (value[plane * rows : (plane + 1) * rows] + rest).astype(BF16)


def join_high_kernel(
    pattern_ref, local_ref, before_hbm, after_hbm, masked_ref, low_ref, out_ref, before, after, total, sem
):
    planes, rows, cols = local_ref.shape
    lows = low_ref.shape[0]
    copies = fetch([before_hbm, after_hbm], [before, after], [sem.at[0], sem.at[1]])
    scale = pattern_ref[0].astype(F32)
    size = total.shape[0] * total.shape[1]
    out_ref[size:, :] = jnp.zeros((out_ref.shape[0] - size, LANES), BF16)
    for plane in range(lows):
        spread(total, plane, lows + planes, low_ref[plane].astype(F32))
    arrive(copies)
    value = dot(before[...].reshape(planes * rows, cols), masked_ref[...])
    for plane in range(planes):
        rest = after[plane].astype(F32) * scale + local_ref[plane].astype(F32)
        spread(total, lows + plane, lows + planes, value[plane * rows : (plane + 1) * rows] + rest)
    for tile in range(total.shape[0]):
        at = slice(tile * total.shape[1], (tile + 1) * total.shape[1])
        out_ref[at, :] = total[tile].astype(BF16)


def unit_pairs(got_ref):
    peers, units, planes, lanes = got_ref.shape
    for first in range(0, units, 2):
        some = range(first, min(first + 2, units))
        yield first, [got_ref[:, unit].reshape(peers * planes, lanes) for unit in some]


def spectrum_kernel(scale, forward_ref, got_ref, out_ref):
    for first, values in unit_pairs(got_ref):
        width = LANES * len(values)
        out_ref[first // 2, :, :width] = dot(forward_ref[...], jnp.concatenate(values, 1)) * scale


def convolve_kernel(forward_ref, inverse_ref, green_ref, got_ref, out_ref):
    peers, _, planes, lanes = got_ref.shape
    half = forward_ref.shape[0] // 2
    for first, values in unit_pairs(got_ref):
        width = LANES * len(values)
        freq = dot(forward_ref[...], jnp.concatenate(values, 1))
        green_re, green_im = green_ref[first // 2, :half, :width], green_ref[first // 2, half:, :width]
        screen_re, screen_im = freq[:half], freq[half:]
        mixed = jnp.concatenate(
            [green_re * screen_re - green_im * screen_im, green_re * screen_im + green_im * screen_re], 0
        )
        result = dot(inverse_ref[...], mixed.astype(BF16)).astype(BF16)
        for at in range(len(values)):
            out_ref[:, first + at] = result[:, at * lanes : (at + 1) * lanes].reshape(peers, planes, lanes)


def unpack_kernel(present_ref, got_ref, out_hbm, turn_ref, ready, sem):
    groups = present_ref.shape[0]
    planes, _, cols = ready.shape
    tiles = cols // LANES
    span = LIVE * RG * planes
    batch = groups // sem.shape[0]
    for tile in range(tiles):
        turn_ref[tile, :span] = got_ref[tile * span : (tile + 1) * span, :].astype(F32)
    copies = []
    slot = jnp.int32(0)
    for group in range(groups):
        rows = slice(group * RG, (group + 1) * RG)
        live = present_ref[group] > 0
        at = pl.multiple_of(slot * RG * planes, RG * planes)
        for tile in range(tiles):
            for plane in range(planes):
                value = turn_ref[tile, pl.ds(at + plane, RG, stride=planes), :]
                value = jnp.where(live, value, 0.0).astype(BF16)
                ready[plane, rows, tile * LANES : (tile + 1) * LANES] = value
        slot = slot + jnp.where(live, 1, 0)
        if group % batch == batch - 1:
            some = slice((group + 1 - batch) * RG, (group + 1) * RG)
            copies += fetch([ready.at[:, some]], [out_hbm.at[:, some]], [sem.at[group // batch]])
    arrive(copies)


def per_device(g_upper, p_diag, p_upper, v_diag, v_upper, v_pattern, element_present):
    peers = lax.axis_size("energy")
    halves, local, _, size, _ = g_upper.shape
    planes = halves * local
    energies = local * peers
    live = LIVE * RG
    flat = live * planes

    def stay(value):
        return pltpu.with_memory_space_constraint(value, pltpu.HBM)

    p_d, p_u = (stay(x.reshape(planes, size, size)) for x in (p_diag, p_upper))
    v_d, v_u = (x.reshape(size, size) for x in (v_diag, v_upper))
    v_d_here, v_u_here = stay(v_d), stay(v_u)

    def near(value):
        return pltpu.with_memory_space_constraint(value, pltpu.VMEM)

    p_d_near, p_u_near, green = (
        near(x.reshape(planes, size, size)) for x in (p_diag, p_upper, g_upper)
    )
    v_d_near, v_u_near = near(v_d), near(v_u)
    present = element_present.reshape(-1)
    groups = present.shape[0]
    tiles = size // LANES
    units = -(-live * tiles // peers)
    routes = peers * units * planes

    idx = pltpu.SMEM((groups,), jnp.int32)
    square = pltpu.VMEM((size, size), F32)
    strip = pltpu.VMEM((live, size), F32)
    total = pltpu.VMEM((size // LANES, flat, LANES), F32)
    big = planes * size * size * 2

    def call(kernel, outs, ins, scratch, units, mib, places=None):
        if places is None:
            places = [vmem() for _ in outs] if isinstance(outs, list) else vmem()
        return pl.pallas_call(
            kernel,
            out_shape=outs,
            in_specs=ins,
            out_specs=places,
            scratch_shapes=scratch,
            compiler_params=pltpu.CompilerParams(vmem_limit_bytes=mib * 2**20),
            cost_estimate=pl.CostEstimate(
                flops=int(units * 2 * planes * live * size * size), bytes_accessed=int(big), transcendentals=0
            ),
        )

    def array(*shape, dtype=BF16):
        return jax.ShapeDtypeStruct(shape, dtype)

    chosen = call(
        prepare_kernel,
        array(live, size),
        [smem()] * 2 + [hbm()],
        [idx, pltpu.VMEM((live, size), BF16), pltpu.SemaphoreType.DMA((LIVE,))],
        8,
        6,
    )(present, v_pattern, v_u_here)
    v_u_prev = shifted(chosen, 1)
    present_next = shifted(present, -1)
    v_d_next = shifted(v_d, -1)
    forward, inverse = tables(energies, peers)

    whole = pltpu.VMEM((planes, size, size), BF16)
    sems = pltpu.SemaphoreType.DMA((2, planes))
    pair = pltpu.SemaphoreType.DMA((2,))
    block = pltpu.VMEM((size, size), BF16)
    inner, turned = call(
        inner_kernel,
        [array(planes, size, size), array(size, size, dtype=F32)],
        [smem()] + [vmem()] * 4,
        [],
        3.2,
        12,
    )(v_pattern, v_d_near, v_u_near, p_d_near, p_u_near)
    half = planes // 2
    parcel = pltpu.VMEM((half, live, size), BF16)
    moving = [pltpu.VMEM((2, half, live, size), BF16), pltpu.SemaphoreType.DMA((2, half // 2))]

    def outward(part, ins, outs, specs, scratch):
        kernel = functools.partial(outward_kernel, part)
        places = [hbm(), hbm()] + [vmem()] * (len(outs) - 2)
        return call(kernel, outs, specs, scratch + moving, 1, 8, places)(*ins)

    leaving = [array(half, live, size)] * 2
    to_next, to_prev, picked = outward(
        0,
        [present_next, turned, v_u_prev, p_u_near, inner],
        leaving + [array(live, size)],
        [smem()] + [vmem()] * 4,
        [idx, strip],
    )
    after, before = [shifted(to_prev, -1)], [shifted(to_next, 1)]
    to_next, to_prev = outward(1, [picked, v_u_prev, p_u_near, inner], leaving, [vmem()] * 4, [])
    after.append(shifted(to_prev, -1))
    before.append(shifted(to_next, 1))

    send_green = call(
        pack_kernel,
        array(routes, LANES),
        [smem(), vmem()],
        [idx, total, pltpu.VMEM((routes, LANES), BF16), pltpu.SemaphoreType.DMA((tiles,))],
        0.3,
        8,
        hbm(),
    )(present, green)
    got_green = routed(send_green.reshape(peers, units, planes, LANES))

    stacked = pltpu.VMEM((flat, size), BF16)
    own = call(
        local_kernel,
        [array(half, live, size)] * 2,
        [smem()] * 2 + [hbm()] * 2 + [vmem()] + [hbm()] * 2,
        [idx, square, strip, strip, stacked, stacked, whole, whole, block, block, sems, pair],
        5,
        16,
    )(present, v_pattern, v_u_here, v_d_here, v_d_next, p_d, p_u)

    green_freq = call(
        functools.partial(spectrum_kernel, 1.0 / (energies * math.sqrt(energies))),
        array(-(-units // 2), 2 * energies, 2 * LANES, dtype=F32),
        [vmem(), vmem()],
        [],
        0.5,
        8,
    )(forward, got_green)

    partial, masked = call(
        join_low_kernel,
        [array(half, live, size), array(size, size)],
        [smem(), vmem()] + [hbm()] * 3,
        [parcel, parcel, block, pltpu.SemaphoreType.DMA((3,))],
        0.5,
        6,
    )(v_pattern, own[0], stay(before[0]), stay(after[0]), v_u_here)
    send = call(
        join_high_kernel,
        array(routes, LANES),
        [smem(), vmem()] + [hbm()] * 2 + [vmem()] * 2,
        [parcel, parcel, total, pair],
        0.5,
        10,
    )(v_pattern, own[1], stay(before[1]), stay(after[1]), masked, partial)
    got = routed(send.reshape(peers, units, planes, LANES))
    result = call(
        convolve_kernel, array(peers, units, planes, LANES), [vmem()] * 4, [], 1, 10
    )(forward, inverse, green_freq, got)
    returned = routed(result).reshape(routes, LANES)

    sigma = call(
        unpack_kernel,
        array(planes, size, size),
        [smem(), vmem()],
        [pltpu.VMEM((tiles, flat + RG * planes, LANES), F32), whole, pltpu.SemaphoreType.DMA((4,))],
        0.3,
        8,
        hbm(),
    )(present, returned)
    return sigma.reshape(halves, local, 1, size, size)


def solution(mesh):
    in_specs = (
        P(None, "energy", "space", None, None),
        P(None, "energy", "space", None, None),
        P(None, "energy", "space", None, None),
        P("space", None, None),
        P("space", None, None),
        P("space"),
        P("space", None),
    )
    out_specs = P(None, "energy", "space", None, None)

    return jax.shard_map(per_device, mesh=mesh, in_specs=in_specs, out_specs=out_specs, check_vma=False)
```

```python
import functools
import math

import jax
import jax.numpy as jnp
import numpy as np
from jax import lax
from jax.experimental import pallas as pl
from jax.experimental.pallas import tpu as pltpu
from jax.sharding import PartitionSpec as P


LIVE = 30
RG = 8
LANES = 128

F32 = jnp.float32
BF16 = jnp.bfloat16


def smem():
    return pl.BlockSpec(memory_space=pltpu.SMEM)


def vmem():
    return pl.BlockSpec(memory_space=pltpu.VMEM)


def hbm():
    return pl.BlockSpec(memory_space=pltpu.HBM)


def shifted(value, steps):
    count = lax.axis_size("space")
    pairs = [(source, (source + steps) % count) for source in range(count)]
    return lax.ppermute(value, "space", pairs)


def routed(value):
    return lax.all_to_all(value, "energy", split_axis=0, concat_axis=0, tiled=True)


def dot(left, right):
    return lax.dot_general(left, right, (((1,), (0,)), ((), ())), preferred_element_type=F32)


def dot_nt(left, right):
    return lax.dot_general(left, right, (((1,), (1,)), ((), ())), preferred_element_type=F32)


def tables(energies, peers):
    local = energies // peers
    src, half, step = np.meshgrid(np.arange(peers), np.arange(2), np.arange(local), indexing="ij")
    time = (src * local + step).reshape(-1)
    half = half.reshape(-1)
    freq = np.arange(energies)
    angles = 2.0 * math.pi / energies * ((freq[:, None] * time[None, :]) % energies)
    cosine, sine = np.cos(angles), np.sin(angles)
    real_part = np.where(half == 0, cosine, sine)
    imag_part = np.where(half == 0, -sine, cosine)
    forward = np.concatenate([real_part, imag_part], 0)
    real_out = np.concatenate([-sine, -cosine], 0).T
    imag_out = np.concatenate([cosine, -sine], 0).T
    inverse = np.where((half == 0)[:, None], real_out, imag_out)
    return jnp.asarray(forward, BF16), jnp.asarray(inverse, BF16)


def fetch(sources, targets, sems):
    copies = [pltpu.make_async_copy(a, b, sem) for a, b, sem in zip(sources, targets, sems)]
    for copy in copies:
        copy.start()
    return copies


def arrive(copies):
    for copy in copies:
        copy.wait()


def spread(dest_ref, plane, planes, value):
    rows = value.shape[0]
    for j in range(value.shape[1] // LANES):
        dest_ref[j, pl.ds(plane, rows, stride=planes), :] = value[:, j * LANES : (j + 1) * LANES]


def live_list(present_ref, idx_ref):
    for slot in range(LIVE):
        idx_ref[slot] = 0
    count = jnp.int32(0)
    for group in range(present_ref.shape[0]):
        idx_ref[count] = group
        count = count + jnp.where(present_ref[group] > 0, 1, 0)
    return count


def pick_rows(idx_ref, source_ref, dest_ref):
    for slot in range(LIVE):
        row = pl.multiple_of(idx_ref[slot] * RG, RG)
        dest_ref[slot * RG : (slot + 1) * RG, :] = source_ref[pl.ds(row, RG), :]


def pack_kernel(present_ref, g_ref, out_hbm, idx_ref, turn_ref, ready, sem):
    planes = g_ref.shape[0]
    tiles, span, _ = turn_ref.shape
    live_list(present_ref, idx_ref)
    copies = []
    for tile in range(tiles):
        cols = slice(tile * LANES, (tile + 1) * LANES)
        for slot in range(LIVE):
            row = pl.multiple_of(idx_ref[slot] * RG, RG)
            for plane in range(planes):
                at = slot * RG * planes + plane
                value = g_ref[plane, pl.ds(row, RG), cols].astype(F32)
                turn_ref[tile, pl.ds(at, RG, stride=planes), :] = value
        ready[tile * span : (tile + 1) * span, :] = turn_ref[tile].astype(BF16)
        end = (tile + 1) * span
        if tile == tiles - 1:
            ready[end:, :] = jnp.zeros((ready.shape[0] - end, LANES), BF16)
            end = ready.shape[0]
        rows = slice(tile * span, end)
        copies += fetch([ready.at[rows]], [out_hbm.at[rows]], [sem.at[tile]])
    arrive(copies)


def inner_kernel(pattern_ref, vd_ref, vu_ref, pd_ref, pu_ref, out_ref, turned_ref):
    scale = pattern_ref[0].astype(F32)
    turned = (vu_ref[...].astype(F32) * scale).T
    turned_ref[...] = turned
    right = jnp.concatenate([vd_ref[...], turned.astype(BF16)], axis=0)
    for plane in range(out_ref.shape[0]):
        left = jnp.concatenate([pd_ref[plane], pu_ref[plane]], axis=1)
        out_ref[plane] = dot(left, right).astype(BF16)


def prepare_kernel(present_ref, pattern_ref, vu_ref, out_ref, idx_ref, wide, picked):
    live_list(present_ref, idx_ref)
    wide[...] = vu_ref[...].astype(F32) * pattern_ref[0].astype(F32)
    pick_rows(idx_ref, wide, picked)
    out_ref[...] = picked[...].astype(BF16)


def outward_kernel(half, *refs):
    if half == 0:
        next_ref, turned_ref, left_ref, pu_ref, inner_ref, to_next, to_prev, picked_ref, idx, picked, ready, sem = refs
    else:
        picked_ref, left_ref, pu_ref, pd_ref, vd_ref, turned_ref, to_next, to_prev, inner_ref, ready, sem = refs
        right = jnp.concatenate([vd_ref[...], turned_ref[...].astype(BF16)], axis=0)
        for plane in range(inner_ref.shape[0]):
            at = plane + inner_ref.shape[0]
            inner_ref[plane] = dot(jnp.concatenate([pd_ref[at], pu_ref[at]], axis=1), right).astype(BF16)
    planes = ready.shape[1]
    left_prev = left_ref[...]
    copies = []
    for way, (right_ref, out_hbm) in enumerate(((inner_ref, to_prev), (pu_ref, to_next))):
        left = left_prev
        if way == 1 and half == 0:
            live_list(next_ref, idx)
            pick_rows(idx, turned_ref, picked)
            left = picked[...].astype(BF16)
            picked_ref[...] = left
        elif way == 1:
            left = picked_ref[...]
        for plane in range(planes):
            at = plane + (half * planes if way == 1 else 0)
            ready[way, plane] = dot(left, right_ref[at]).astype(BF16)
            if plane % 2 == 1:
                some = slice(plane - 1, plane + 1)
                copies += fetch([ready.at[way, some]], [out_hbm.at[some]], [sem.at[way, plane // 2]])
    arrive(copies)


def local_kernel(
    present_ref,
    pattern_ref,
    vu_hbm,
    vd_hbm,
    vd_next_ref,
    pd_hbm,
    pu_hbm,
    low_ref,
    high_ref,
    idx_ref,
    wide,
    picked_u,
    picked_d,
    same,
    one_up,
    pd_ref,
    pu_ref,
    vd_ref,
    vu_ref,
    sem,
    v_sem,
):
    planes = pu_ref.shape[0]
    rows = LIVE * RG
    small = fetch([vd_hbm, vu_hbm], [vd_ref, vu_ref], [v_sem.at[0], v_sem.at[1]])
    copies = [
        fetch(
            [pd_hbm.at[plane], pu_hbm.at[plane]],
            [pd_ref.at[plane], pu_ref.at[plane]],
            [sem.at[0, plane], sem.at[1, plane]],
        )
        for plane in range(planes)
    ]
    live_list(present_ref, idx_ref)
    arrive(small)
    wide[...] = vu_ref[...].astype(F32) * pattern_ref[0].astype(F32)
    masked = wide[...].astype(BF16)
    pick_rows(idx_ref, wide, picked_u)
    wide[...] = vd_ref[...].astype(F32)
    pick_rows(idx_ref, wide, picked_d)
    left_u = picked_u[...].astype(BF16)
    left_d = picked_d[...].astype(BF16)
    for plane in range(planes):
        arrive(copies[plane])
        at = slice(plane * rows, (plane + 1) * rows)
        same[at] = (dot(left_d, pd_ref[plane]) + dot_nt(left_u, pu_ref[plane])).astype(BF16)
        one_up[at] = dot(left_d, pu_ref[plane]).astype(BF16)
    for plane in range(planes):
        at = slice(plane * rows, (plane + 1) * rows)
        value = dot(same[at], masked) + dot(one_up[at], vd_next_ref[...])
        if plane < planes // 2:
            value = value + picked_u[...]
        out_ref = low_ref if plane < planes // 2 else high_ref
        out_ref[plane % (planes // 2)] = value.astype(BF16)


def join_low_kernel(
    pattern_ref, local_ref, before_hbm, after_hbm, vu_hbm, out_ref, masked_ref, before, after, vu_ref, sem
):
    planes, rows, cols = local_ref.shape
    scale = pattern_ref[0].astype(F32)
    copies = fetch([vu_hbm, before_hbm, after_hbm], [vu_ref, before, after], [sem.at[0], sem.at[1], sem.at[2]])
    arrive(copies)
    masked_ref[...] = (vu_ref[...].astype(F32) * scale).astype(BF16)
    value = dot(before[...].reshape(planes * rows, cols), masked_ref[...])
    for plane in range(planes):
        rest = after[plane].astype(F32) * scale + local_ref[plane].astype(F32)
        out_ref[plane] = (value[plane * rows : (plane + 1) * rows] + rest).astype(BF16)


def join_high_kernel(
    pattern_ref, local_ref, before_hbm, after_hbm, masked_ref, low_ref, out_ref, before, after, total, sem
):
    planes, rows, cols = local_ref.shape
    lows = low_ref.shape[0]
    copies = fetch([before_hbm, after_hbm], [before, after], [sem.at[0], sem.at[1]])
    scale = pattern_ref[0].astype(F32)
    size = total.shape[0] * total.shape[1]
    out_ref[size:, :] = jnp.zeros((out_ref.shape[0] - size, LANES), BF16)
    for plane in range(lows):
        spread(total, plane, lows + planes, low_ref[plane].astype(F32))
    arrive(copies)
    value = dot(before[...].reshape(planes * rows, cols), masked_ref[...])
    for plane in range(planes):
        rest = after[plane].astype(F32) * scale + local_ref[plane].astype(F32)
        spread(total, lows + plane, lows + planes, value[plane * rows : (plane + 1) * rows] + rest)
    for tile in range(total.shape[0]):
        at = slice(tile * total.shape[1], (tile + 1) * total.shape[1])
        out_ref[at, :] = total[tile].astype(BF16)


def unit_pairs(got_ref):
    peers, units, planes, lanes = got_ref.shape
    for first in range(0, units, 2):
        some = range(first, min(first + 2, units))
        yield first, [got_ref[:, unit].reshape(peers * planes, lanes) for unit in some]


def spectrum_kernel(scale, forward_ref, got_ref, out_ref):
    for first, values in unit_pairs(got_ref):
        width = LANES * len(values)
        out_ref[first // 2, :, :width] = dot(forward_ref[...], jnp.concatenate(values, 1)) * scale


def convolve_kernel(forward_ref, inverse_ref, green_ref, got_ref, out_ref):
    peers, _, planes, lanes = got_ref.shape
    half = forward_ref.shape[0] // 2
    for first, values in unit_pairs(got_ref):
        width = LANES * len(values)
        freq = dot(forward_ref[...], jnp.concatenate(values, 1))
        green_re, green_im = green_ref[first // 2, :half, :width], green_ref[first // 2, half:, :width]
        screen_re, screen_im = freq[:half], freq[half:]
        mixed = jnp.concatenate(
            [green_re * screen_re - green_im * screen_im, green_re * screen_im + green_im * screen_re], 0
        )
        result = dot(inverse_ref[...], mixed.astype(BF16)).astype(BF16)
        for at in range(len(values)):
            out_ref[:, first + at] = result[:, at * lanes : (at + 1) * lanes].reshape(peers, planes, lanes)


def unpack_kernel(present_ref, got_ref, out_hbm, turn_ref, ready, sem):
    groups = present_ref.shape[0]
    planes, _, cols = ready.shape
    tiles = cols // LANES
    span = LIVE * RG * planes
    batch = groups // sem.shape[0]
    for tile in range(tiles):
        turn_ref[tile, :span] = got_ref[tile * span : (tile + 1) * span, :].astype(F32)
    copies = []
    slot = jnp.int32(0)
    for group in range(groups):
        rows = slice(group * RG, (group + 1) * RG)
        live = present_ref[group] > 0
        at = pl.multiple_of(slot * RG * planes, RG * planes)
        for tile in range(tiles):
            for plane in range(planes):
                value = turn_ref[tile, pl.ds(at + plane, RG, stride=planes), :]
                value = jnp.where(live, value, 0.0).astype(BF16)
                ready[plane, rows, tile * LANES : (tile + 1) * LANES] = value
        slot = slot + jnp.where(live, 1, 0)
        if group % batch == batch - 1:
            some = slice((group + 1 - batch) * RG, (group + 1) * RG)
            copies += fetch([ready.at[:, some]], [out_hbm.at[:, some]], [sem.at[group // batch]])
    arrive(copies)


def per_device(g_upper, p_diag, p_upper, v_diag, v_upper, v_pattern, element_present):
    peers = lax.axis_size("energy")
    halves, local, _, size, _ = g_upper.shape
    planes = halves * local
    energies = local * peers
    live = LIVE * RG
    flat = live * planes

    def stay(value):
        return pltpu.with_memory_space_constraint(value, pltpu.HBM)

    p_d, p_u = (stay(x.reshape(planes, size, size)) for x in (p_diag, p_upper))
    v_d, v_u = (x.reshape(size, size) for x in (v_diag, v_upper))
    v_d_here, v_u_here = stay(v_d), stay(v_u)

    def near(value):
        return pltpu.with_memory_space_constraint(value, pltpu.VMEM)

    p_d_near, p_u_near, green = (
        near(x.reshape(planes, size, size)) for x in (p_diag, p_upper, g_upper)
    )
    v_d_near, v_u_near = near(v_d), near(v_u)
    present = element_present.reshape(-1)
    groups = present.shape[0]
    tiles = size // LANES
    units = -(-live * tiles // peers)
    routes = peers * units * planes

    idx = pltpu.SMEM((groups,), jnp.int32)
    square = pltpu.VMEM((size, size), F32)
    strip = pltpu.VMEM((live, size), F32)
    total = pltpu.VMEM((size // LANES, flat, LANES), F32)
    big = planes * size * size * 2

    def call(kernel, outs, ins, scratch, units, mib, places=None):
        if places is None:
            places = [vmem() for _ in outs] if isinstance(outs, list) else vmem()
        return pl.pallas_call(
            kernel,
            out_shape=outs,
            in_specs=ins,
            out_specs=places,
            scratch_shapes=scratch,
            compiler_params=pltpu.CompilerParams(vmem_limit_bytes=mib * 2**20),
            cost_estimate=pl.CostEstimate(
                flops=int(units * 2 * planes * live * size * size), bytes_accessed=int(big), transcendentals=0
            ),
        )

    def array(*shape, dtype=BF16):
        return jax.ShapeDtypeStruct(shape, dtype)

    chosen = call(
        prepare_kernel, array(live, size), [smem()] * 2 + [vmem()], [idx, square, strip], 8, 6
    )(present, v_pattern, v_u)
    v_u_prev = shifted(chosen, 1)
    present_next = shifted(present, -1)
    v_d_next = shifted(v_d, -1)
    forward, inverse = tables(energies, peers)

    whole = pltpu.VMEM((planes, size, size), BF16)
    sems = pltpu.SemaphoreType.DMA((2, planes))
    pair = pltpu.SemaphoreType.DMA((2,))
    block = pltpu.VMEM((size, size), BF16)
    inner, turned = call(
        inner_kernel,
        [array(planes // 2, size, size), array(size, size, dtype=F32)],
        [smem()] + [vmem()] * 4,
        [],
        3.2,
        12,
    )(v_pattern, v_d_near, v_u_near, p_d_near, p_u_near)
    half = planes // 2
    parcel = pltpu.VMEM((half, live, size), BF16)
    moving = [pltpu.VMEM((2, half, live, size), BF16), pltpu.SemaphoreType.DMA((2, half // 2))]

    def outward(part, ins, outs, specs, scratch):
        kernel = functools.partial(outward_kernel, part)
        places = [hbm(), hbm()] + [vmem()] * (len(outs) - 2)
        return call(kernel, outs, specs, scratch + moving, 1, 8, places)(*ins)

    leaving = [array(half, live, size)] * 2
    to_next, to_prev, picked = outward(
        0,
        [present_next, turned, v_u_prev, p_u_near, inner],
        leaving + [array(live, size)],
        [smem()] + [vmem()] * 4,
        [idx, strip],
    )
    after, before = [shifted(to_prev, -1)], [shifted(to_next, 1)]
    to_next, to_prev = outward(
        1,
        [picked, v_u_prev, p_u_near, p_d_near, v_d_near, turned],
        leaving,
        [vmem()] * 6,
        [pltpu.VMEM((half, size, size), BF16)],
    )
    after.append(shifted(to_prev, -1))
    before.append(shifted(to_next, 1))

    send_green = call(
        pack_kernel,
        array(routes, LANES),
        [smem(), vmem()],
        [idx, total, pltpu.VMEM((routes, LANES), BF16), pltpu.SemaphoreType.DMA((tiles,))],
        0.3,
        8,
        hbm(),
    )(present, green)
    got_green = routed(send_green.reshape(peers, units, planes, LANES))

    stacked = pltpu.VMEM((flat, size), BF16)
    own = call(
        local_kernel,
        [array(half, live, size)] * 2,
        [smem()] * 2 + [hbm()] * 2 + [vmem()] + [hbm()] * 2,
        [idx, square, strip, strip, stacked, stacked, whole, whole, block, block, sems, pair],
        5,
        16,
    )(present, v_pattern, v_u_here, v_d_here, v_d_next, p_d, p_u)

    green_freq = call(
        functools.partial(spectrum_kernel, 1.0 / (energies * math.sqrt(energies))),
        array(-(-units // 2), 2 * energies, 2 * LANES, dtype=F32),
        [vmem(), vmem()],
        [],
        0.5,
        8,
    )(forward, got_green)

    partial, masked = call(
        join_low_kernel,
        [array(half, live, size), array(size, size)],
        [smem(), vmem()] + [hbm()] * 3,
        [parcel, parcel, block, pltpu.SemaphoreType.DMA((3,))],
        0.5,
        6,
    )(v_pattern, own[0], stay(before[0]), stay(after[0]), v_u_here)
    send = call(
        join_high_kernel,
        array(routes, LANES),
        [smem(), vmem()] + [hbm()] * 2 + [vmem()] * 2,
        [parcel, parcel, total, pair],
        0.5,
        10,
    )(v_pattern, own[1], stay(before[1]), stay(after[1]), masked, partial)
    got = routed(send.reshape(peers, units, planes, LANES))
    result = call(
        convolve_kernel, array(peers, units, planes, LANES), [vmem()] * 4, [], 1, 10
    )(forward, inverse, green_freq, got)
    returned = routed(result).reshape(routes, LANES)

    sigma = call(
        unpack_kernel,
        array(planes, size, size),
        [smem(), vmem()],
        [pltpu.VMEM((tiles, flat + RG * planes, LANES), F32), whole, pltpu.SemaphoreType.DMA((4,))],
        0.3,
        8,
        hbm(),
    )(present, returned)
    return sigma.reshape(halves, local, 1, size, size)


def solution(mesh):
    in_specs = (
        P(None, "energy", "space", None, None),
        P(None, "energy", "space", None, None),
        P(None, "energy", "space", None, None),
        P("space", None, None),
        P("space", None, None),
        P("space"),
        P("space", None),
    )
    out_specs = P(None, "energy", "space", None, None)

    return jax.shard_map(per_device, mesh=mesh, in_specs=in_specs, out_specs=out_specs, check_vma=False)
```
